32 devices in a mesh: fsdp: 32 (over z, y, x, core).
Axes of the slice: x: 2, y: 2, z: 4, core: 2. Of those that a mesh axis runs over, the one named last changes fastest.
Arguments:
- layer_input: bfloat16 [96, 288, 768], P('fsdp'), may hold values from -6 to 6
- segments: int32 [96, 288], P('fsdp'), may hold values from 0 to 8, as said below
- cotangent: bfloat16 [96, 288, 768], P('fsdp'), may hold values from -6 to 6
- pre_gain: float32 [768], P('fsdp'), may hold values from 0.5 to 1.5
- pre_shift: float32 [768], P('fsdp'), may hold values from -2 to 2
- w_qkv: float32 [768, 2304], P('fsdp'), may hold values from -0.21875 to 0.21875
- b_query: float32 [768], P('fsdp'), may hold values from -3 to 3
- b_value: float32 [768], P('fsdp'), may hold values from -3 to 3
- w_out: float32 [768, 768], P('fsdp'), may hold values from -1.25 to 1.25
- b_out: float32 [768], P('fsdp'), may hold values from -3 to 3
- mid_gain: float32 [768], P('fsdp'), may hold values from 0.5 to 1.5
- mid_shift: float32 [768], P('fsdp'), may hold values from -2 to 2
- w_up: float32 [768, 3072], P('fsdp'), may hold values from -0.21875 to 0.21875
- b_up: float32 [3072], P('fsdp'), may hold values from -3 to 3
- w_down: float32 [3072, 768], P('fsdp'), may hold values from -0.109375 to 0.109375
- b_down: float32 [768], P('fsdp'), may hold values from -3 to 3
Outputs:
- layer_output: bfloat16 [96, 288, 768], P('fsdp')
- grad_input: bfloat16 [96, 288, 768], P('fsdp')
- grad_pre_gain: float32 [768], P('fsdp')
- grad_pre_shift: float32 [768], P('fsdp')
- grad_w_qkv: float32 [768, 2304], P('fsdp')
- grad_b_query: float32 [768], P('fsdp')
- grad_b_value: float32 [768], P('fsdp')
- grad_w_out: float32 [768, 768], P('fsdp')
- grad_b_out: float32 [768], P('fsdp')
- grad_mid_gain: float32 [768], P('fsdp')
- grad_mid_shift: float32 [768], P('fsdp')
- grad_w_up: float32 [768, 3072], P('fsdp')
- grad_b_up: float32 [3072], P('fsdp')
- grad_w_down: float32 [3072, 768], P('fsdp')
- grad_b_down: float32 [768], P('fsdp')
The draws below stay inside these ranges and needn't reach their ends.
Inputs may be any that keep to these rules, and one draw needn't show every extreme that they name: `segments`: each row holds 8 or 7 images of 36 slots each, in slot order and numbered from 1; the remaining slots of a row are padding (0).
All inputs are finite; a program needn't handle non-finite values.
Results may differ from the reference program's by a relative error of at most 0.012.
The reference program's roundings to bfloat16 on the way count: a program that leaves them out, or rounds other values in their place, can miss the bound.
Values may be sent and summed in bfloat16 or wider, within the bound.
No kernel may reach another device: no remote copies, remote signals or barrier semaphores. Data moves between devices by JAX's collectives and lax.ppermute only.
A program may use at most 192 MiB of HBM per device.

```python
import jax
import jax.numpy as jnp
from jax import lax

D = 768
HEAD_DIM = 64
FF = 3072
PATCHES = 36
PACK = 8
SLOTS = 288
ROWS = 96


def draw_segments(key, part):
    picks = jax.random.randint(key, (ROWS,), 0, 43)
    row_index = jnp.arange(ROWS)
    shorter = ((picks == 0) | (row_index == ROWS - 1)) & (row_index != 0)
    images = jnp.where(shorter, PACK - 1, PACK).astype(jnp.int32)
    placed = (jnp.arange(SLOTS) // PATCHES).astype(jnp.int32)
    number = placed + 1
    return jnp.where(placed[None, :] < images[:, None], number[None, :], 0).astype(jnp.int32)


def steps_of(stream_key, extent, cuts, least, top_value):
    level, own = 1.0, jax.random.fold_in(stream_key, 6)
    for dim, shards_of in cuts:
        heights = jnp.exp(jax.random.uniform(jax.random.fold_in(own, dim), (shards_of,), jnp.float32, least / len(cuts), top_value / len(cuts)))
        level = level * jnp.repeat(heights, extent[dim] // shards_of).reshape([-1 if axis == dim else 1 for axis in range(len(extent))])
    return level


def normal_values(key, extent, width, bound, cuts=(), held_as=jnp.bfloat16):
    values = width * jax.random.normal(key, extent, jnp.float32)
    if cuts:
        values = values * steps_of(key, extent, cuts, -0.22, 0.18)
    return jnp.clip(values, -bound, bound).astype(held_as)


def setup_inputs(seed: int = 0) -> dict:
    seeds = jax.random.split(jax.random.key(seed), 17)
    layer_input = normal_values(seeds[0], (ROWS, SLOTS, D), 1.0, 6.0, ((0, 32),))
    segments = draw_segments(jax.random.fold_in(seeds[16], 71), 0)
    cotangent = normal_values(seeds[2], (ROWS, SLOTS, D), 1.0, 6.0, ((0, 32),))
    pre_gain = jnp.clip(1.0 + 0.1 * jax.random.normal(seeds[3], (D,), jnp.float32), 0.5, 1.5)
    pre_shift = normal_values(seeds[4], (D,), 0.3, 2.0, ((0, 32),), jnp.float32)
    w_qkv = normal_values(seeds[5], (D, 3 * D), D ** -0.5, 0.21875, ((0, 32),), jnp.float32)
    b_query = normal_values(seeds[6], (D,), 0.5, 3.0, ((0, 32),), jnp.float32)
    b_value = normal_values(seeds[7], (D,), 0.5, 3.0, ((0, 32),), jnp.float32)
    w_out = normal_values(seeds[8], (D, D), (D // PATCHES) ** -0.5, 1.25, ((0, 32),), jnp.float32)
    b_out = normal_values(seeds[9], (D,), 0.5, 3.0, ((0, 32),), jnp.float32)
    mid_gain = jnp.clip(1.0 + 0.1 * jax.random.normal(seeds[10], (D,), jnp.float32), 0.5, 1.5)
    mid_shift = normal_values(seeds[11], (D,), 0.3, 2.0, ((0, 32),), jnp.float32)
    w_up = normal_values(seeds[12], (D, FF), D ** -0.5, 0.21875, ((0, 32),), jnp.float32)
    b_up = normal_values(seeds[13], (FF,), 0.5, 3.0, ((0, 32),), jnp.float32)
    w_down = normal_values(seeds[14], (FF, D), FF ** -0.5, 0.109375, ((0, 32),), jnp.float32)
    b_down = normal_values(seeds[15], (D,), 0.5, 3.0, ((0, 32),), jnp.float32)
    return dict(layer_input=layer_input, segments=segments, cotangent=cotangent, pre_gain=pre_gain, pre_shift=pre_shift, w_qkv=w_qkv, b_query=b_query, b_value=b_value, w_out=w_out, b_out=b_out, mid_gain=mid_gain, mid_shift=mid_shift, w_up=w_up, b_up=b_up, w_down=w_down, b_down=b_down)


@jax.custom_vjp
def low(v):
    return lax.optimization_barrier(v.astype(jnp.bfloat16)).astype(jnp.float32)

@jax.custom_vjp
def low_back(v):
    return v

def low_keep(v):
    return (low(v), None)

def low_pass(kept, grad):
    return (grad,)

def back_keep(v):
    return (v, None)

def back_low(kept, grad):
    return (low(grad),)
low.defvjp(low_keep, low_pass)
low_back.defvjp(back_keep, back_low)
EPSILON = 1e-06
HIGHEST = lax.Precision.HIGHEST

def round_both(value):
    return low_back(low(value))

def norm_layer(value, gain, shift):
    average = lax.optimization_barrier(jnp.mean(value, axis=-1, keepdims=True))
    centred = value - average
    spread = lax.optimization_barrier(jnp.mean(centred * centred, axis=-1, keepdims=True))
    return centred * lax.rsqrt(spread + EPSILON) * gain + shift

def gelu_exact(value):
    return jax.nn.gelu(value, approximate=False)

def layer(inputs, segments, params):
    pre_gain, pre_shift, w_qkv, b_query, b_value, w_out, b_out, mid_gain, mid_shift, w_up, b_up, w_down, b_down = [low(item) for item in params]
    row_count, slot_count, model_width = inputs.shape
    head_count = model_width // HEAD_DIM
    first = low(norm_layer(inputs, pre_gain, pre_shift))
    qkv_bias = jnp.concatenate([b_query, jnp.zeros((model_width,), jnp.float32), b_value])
    qkv = round_both(jnp.einsum('rsd,de->rse', first, w_qkv, precision=HIGHEST) + qkv_bias)
    queries = qkv[..., :model_width].reshape(row_count, slot_count, head_count, HEAD_DIM)
    key_heads = qkv[..., model_width:2 * model_width].reshape(row_count, slot_count, head_count, HEAD_DIM)
    value_heads = qkv[..., 2 * model_width:].reshape(row_count, slot_count, head_count, HEAD_DIM)
    scores = low_back(jnp.einsum('rqhe,rkhe->rhqk', queries, key_heads, precision=HIGHEST) * HEAD_DIM ** (-0.5))
    matching = segments[:, :, None] == segments[:, None, :]
    occupied = (segments > 0)[:, :, None]
    diagonal = (lax.broadcasted_iota(jnp.int32, (slot_count, slot_count), 0) == lax.broadcasted_iota(jnp.int32, (slot_count, slot_count), 1))[None]
    allowed = (matching & occupied | diagonal)[:, None]
    masked = jnp.where(allowed, scores, -1000000000.0)
    highest = lax.optimization_barrier(jnp.max(masked, axis=-1, keepdims=True))
    expd = jnp.exp(masked - highest)
    probs = expd / lax.optimization_barrier(jnp.sum(expd, axis=-1, keepdims=True))
    context = round_both(jnp.einsum('rhqk,rkhe->rqhe', low(probs), value_heads, precision=HIGHEST).reshape(row_count, slot_count, model_width))
    attention = low_back(jnp.einsum('rsd,de->rse', context, w_out, precision=HIGHEST) + b_out)
    middle = inputs + attention
    second = low(norm_layer(middle, mid_gain, mid_shift))
    hidden = low_back(jnp.einsum('rsd,df->rsf', second, w_up, precision=HIGHEST) + b_up)
    activated = low(gelu_exact(hidden))
    branch = low_back(jnp.einsum('rsf,fd->rsd', activated, w_down, precision=HIGHEST) + b_down)
    return middle + branch

def reference(layer_input, segments, cotangent, pre_gain, pre_shift, w_qkv, b_query, b_value, w_out, b_out, mid_gain, mid_shift, w_up, b_up, w_down, b_down):
    params = tuple((item.astype(jnp.float32) for item in (pre_gain, pre_shift, w_qkv, b_query, b_value, w_out, b_out, mid_gain, mid_shift, w_up, b_up, w_down, b_down)))
    group_rows = 8
    groups = ROWS // group_rows
    input_groups = layer_input.astype(jnp.float32).reshape(groups, group_rows, SLOTS, D)
    segment_groups = segments.reshape(groups, group_rows, SLOTS)
    grad_groups = cotangent.astype(jnp.float32).reshape(groups, group_rows, SLOTS, D)

    def one_group(summed, pieces):
        inputs, segs, upstream = pieces
        result, pull_back = jax.vjp(lambda value, weights: layer(value, segs, weights), inputs, params)
        grad_value, grad_params = pull_back(upstream)
        summed = jax.tree.map(lambda left, right: left + right, summed, grad_params)
        return (summed, (result.astype(jnp.bfloat16), grad_value.astype(jnp.bfloat16)))
    start = tuple((jnp.zeros_like(item) for item in params))
    summed, (results, grads) = lax.scan(one_group, start, (input_groups, segment_groups, grad_groups))
    return (results.reshape(ROWS, SLOTS, D), grads.reshape(ROWS, SLOTS, D), summed[0], summed[1], summed[2], summed[3], summed[4], summed[5], summed[6], summed[7], summed[8], summed[9], summed[10], summed[11], summed[12])
```

```python
import jax
import jax.numpy as jnp
from jax import lax
from jax.experimental import pallas as pl
from jax.experimental.pallas import tpu as pltpu
from jax.sharding import PartitionSpec as P

HEAD_DIM = 64
PATCHES = 36
EPSILON = 1e-06
AXIS = "fsdp"


def split_bits(count):
    bits = count.bit_length() - 1
    plane = min(bits - 1, 2) if bits <= 5 else min(bits - 1, 4)
    return 2, 1 << plane, 1 << (bits - 1 - plane), plane + 1


def swap(value, mask, count):
    return lax.ppermute(value, AXIS, [(i, i ^ mask) for i in range(count)])


def my_id():
    return lax.axis_index(AXIS).astype(jnp.int32)[None]


def gather_blocks(shard, count):
    _, planes, depth, zbit = split_bits(count)
    own = shard[None]
    column = jnp.concatenate([own] + [swap(own, m << zbit, count) for m in range(1, depth)], axis=0)
    plane = [column] + [swap(column, q << 1, count) for q in range(1, planes)]
    return plane + [swap(piece, 1, count) for piece in plane]


def lay_out(pieces, count):
    _, planes, depth, zbit = split_bits(count)
    block = pieces[0].shape[1:]

    def body(id_ref, *refs):
        sources, out, sems = refs[: len(pieces)], refs[-2], refs[-1]
        copies = []
        for index, source in enumerate(sources):
            c, q = index // planes, index % planes
            for m in range(depth):
                target = id_ref[0] ^ (c | q << 1 | m << zbit)
                copy = pltpu.make_async_copy(
                    source.at[m], out.at[target], sems.at[index * depth + m]
                )
                copy.start()
                copies.append(copy)
        for copy in copies:
            copy.wait()

    return pl.pallas_call(
        body,
        out_shape=jax.ShapeDtypeStruct((count,) + block, pieces[0].dtype),
        in_specs=[pl.BlockSpec(memory_space=pltpu.SMEM)]
        + [pl.BlockSpec(memory_space=pl.ANY)] * len(pieces),
        out_specs=pl.BlockSpec(memory_space=pltpu.VMEM),
        scratch_shapes=[pltpu.SemaphoreType.DMA((count,))],
        name="lay_out",
    )(my_id(), *pieces)


def gather_rows(shard, count):
    full = lay_out(gather_blocks(shard, count), count)
    return full.reshape((count * shard.shape[0],) + shard.shape[1:])


def relative(parts, count):
    _, planes, depth, zbit = split_bits(count)
    rows = parts[0].shape[1]
    width = sum(part.shape[2] for part in parts)
    half = (planes, depth, rows, width)

    def body(id_ref, *refs):
        sources, keep, send, sems = refs[: len(parts)], refs[-3], refs[-2], refs[-1]
        copies = []
        for c, out in enumerate((keep, send)):
            for q in range(planes):
                for m in range(depth):
                    owner = id_ref[0] ^ (c | q << 1 | m << zbit)
                    start = 0
                    for source in sources:
                        copy = pltpu.make_async_copy(
                            source.at[owner],
                            out.at[q, m, :, pl.ds(start, source.shape[2])],
                            sems.at[len(copies)],
                        )
                        copy.start()
                        copies.append(copy)
                        start += source.shape[2]
        for copy in copies:
            copy.wait()

    return pl.pallas_call(
        body,
        out_shape=(jax.ShapeDtypeStruct(half, parts[0].dtype),) * 2,
        in_specs=[pl.BlockSpec(memory_space=pltpu.SMEM)]
        + [pl.BlockSpec(memory_space=pl.ANY)] * len(parts),
        out_specs=(pl.BlockSpec(memory_space=pltpu.VMEM),) * 2,
        scratch_shapes=[pltpu.SemaphoreType.DMA((count * len(parts),))],
        name="relative",
    )(my_id(), *parts)


def wide(value):
    return value.astype(jnp.float32)


def low(value):
    return value.astype(jnp.bfloat16)


def reduce_blocks(parts, count):
    _, planes, depth, zbit = split_bits(count)
    keep, send = relative(parts, count)
    other = swap(send, 1, count)
    plane = [low(wide(keep[q]) + wide(other[q])) for q in range(planes)]
    column = wide(plane[0])
    for arrived in [swap(plane[q], q << 1, count) for q in range(1, planes)]:
        column = column + wide(arrived)
    column = low(column)
    total = wide(column[0])
    for arrived in [swap(column[m], m << zbit, count) for m in range(1, depth)]:
        total = total + wide(arrived)
    return total


def sum_all(value, count):
    _, planes, depth, zbit = split_bits(count)
    value = value + swap(value, 1, count)
    for arrived in [swap(value, q << 1, count) for q in range(1, planes)]:
        value = value + arrived
    total = value
    for arrived in [swap(value, m << zbit, count) for m in range(1, depth)]:
        total = total + arrived
    return total


def place(value, count):
    whole = jnp.zeros((count * value.shape[0],), value.dtype)
    return lax.dynamic_update_slice(whole, value, (lax.axis_index(AXIS) * value.shape[0],))


def norm_layer(value, gain, shift):
    average = jnp.mean(value, axis=-1, keepdims=True)
    centred = value - average
    spread = jnp.mean(centred * centred, axis=-1, keepdims=True)
    return centred * lax.rsqrt(spread + EPSILON) * gain + shift


def gelu_exact(value):
    return jax.nn.gelu(value, approximate=False)


def column_sums(value):
    return jnp.sum(value.astype(jnp.float32), axis=0)


def shards(
    layer_input,
    segments,
    cotangent,
    pre_gain,
    pre_shift,
    w_qkv,
    b_query,
    b_value,
    w_out,
    b_out,
    mid_gain,
    mid_shift,
    w_up,
    b_up,
    w_down,
    b_down,
):
    row_count, slot_count, model_width = layer_input.shape
    head_count = model_width // HEAD_DIM
    tokens = row_count * slot_count
    images = slot_count // PATCHES
    scaling = HEAD_DIM ** (-0.5)
    tiled = (row_count, images, PATCHES, head_count, HEAD_DIM)
    count = model_width // pre_gain.shape[0]
    small = [pre_gain, pre_shift, b_query, b_value, b_out, mid_gain, mid_shift, b_down]
    vectors = [place(low(item), count) for item in small]
    wider = place(low(b_up), count).reshape(-1, model_width)
    vectors = sum_all(jnp.concatenate([jnp.stack(vectors), wider]), count)
    gain_one, shift_one, query_bias, value_bias, out_bias, gain_two, shift_two, down_bias = [
        vectors[i] for i in range(8)
    ]
    up_bias = vectors[8:].reshape(-1)
    first_weights = gather_rows(jnp.concatenate([low(w_qkv), low(w_out)], axis=1), count)
    qkv_weight = first_weights[:, : 3 * model_width]
    out_weight = first_weights[:, 3 * model_width :]
    up_weight = gather_rows(low(w_up), count)
    down_weight = gather_rows(low(w_down), count)
    inputs = layer_input.astype(jnp.float32).reshape(tokens, model_width)
    normed_one, norm_back_one = jax.vjp(
        norm_layer, inputs, gain_one.astype(jnp.float32), shift_one.astype(jnp.float32)
    )
    first = normed_one.astype(jnp.bfloat16)
    qkv_bias = jnp.concatenate(
        [
            query_bias.astype(jnp.float32),
            jnp.zeros((model_width,), jnp.float32),
            value_bias.astype(jnp.float32),
        ]
    )
    qkv = (jnp.dot(first, qkv_weight, preferred_element_type=jnp.float32) + qkv_bias).astype(
        jnp.bfloat16
    )
    queries = qkv[:, :model_width].reshape(tiled)
    key_heads = qkv[:, model_width : 2 * model_width].reshape(tiled)
    value_heads = qkv[:, 2 * model_width :].reshape(tiled)
    image_segs = segments.reshape(row_count, images, PATCHES)
    matching = image_segs[:, :, :, None] == image_segs[:, :, None, :]
    occupied = (image_segs > 0)[:, :, :, None]
    diagonal = (
        lax.broadcasted_iota(jnp.int32, (PATCHES, PATCHES), 0)
        == lax.broadcasted_iota(jnp.int32, (PATCHES, PATCHES), 1)
    )[None, None]
    allowed = (matching & occupied | diagonal)[:, :, None]

    def masked_scores():
        raw = (
            jnp.einsum("rnqhe,rnkhe->rnhqk", queries, key_heads, preferred_element_type=jnp.float32)
            * scaling
        )
        return jnp.where(allowed, raw, -1000000000.0)

    scores = masked_scores()
    highest = jnp.max(scores, axis=-1, keepdims=True)
    log_total = highest + jnp.log(jnp.sum(jnp.exp(scores - highest), axis=-1, keepdims=True))
    probs_low = jnp.exp(scores - log_total).astype(jnp.bfloat16)
    context = jnp.einsum(
        "rnhqk,rnkhe->rnqhe", probs_low, value_heads, preferred_element_type=jnp.float32
    )
    context_low = context.reshape(tokens, model_width).astype(jnp.bfloat16)
    attention = jnp.dot(
        context_low, out_weight, preferred_element_type=jnp.float32
    ) + out_bias.astype(jnp.float32)
    middle = inputs + attention
    normed_two, norm_back_two = jax.vjp(
        norm_layer, middle, gain_two.astype(jnp.float32), shift_two.astype(jnp.float32)
    )
    second = normed_two.astype(jnp.bfloat16)
    hidden = jnp.dot(second, up_weight, preferred_element_type=jnp.float32) + up_bias.astype(
        jnp.float32
    )
    activated, gelu_back = jax.vjp(gelu_exact, hidden)
    activated_low = activated.astype(jnp.bfloat16)
    branch = jnp.dot(
        activated_low, down_weight, preferred_element_type=jnp.float32
    ) + down_bias.astype(jnp.float32)
    result = (middle + branch).astype(jnp.bfloat16).reshape(row_count, slot_count, model_width)
    up_again, down_again = up_weight, down_weight
    upstream = cotangent.astype(jnp.float32).reshape(tokens, model_width)
    grad_branch = cotangent.reshape(tokens, model_width)
    grad_down = jnp.einsum(
        "tf,td->fd", activated_low, grad_branch, preferred_element_type=jnp.float32
    )
    grad_down_bias = column_sums(grad_branch)
    grad_act = jnp.einsum("td,fd->tf", grad_branch, down_again, preferred_element_type=jnp.float32)
    grad_hidden = gelu_back(grad_act)[0].astype(jnp.bfloat16)
    grad_up = jnp.einsum("td,tf->df", second, grad_hidden, preferred_element_type=jnp.float32)
    grad_up_bias = column_sums(grad_hidden)
    grad_second = jnp.einsum("tf,df->td", grad_hidden, up_again, preferred_element_type=jnp.float32)
    grad_mid_norm, grad_gain_two, grad_shift_two = norm_back_two(grad_second)
    grad_middle = upstream + grad_mid_norm
    blocks = lambda value: low(value).reshape(count, value.shape[0] // count, value.shape[1])
    up_total = reduce_blocks([blocks(grad_up)], count)
    down_total = reduce_blocks([blocks(grad_down)], count)
    qkv_again, out_again = qkv_weight, out_weight
    grad_attention = grad_middle.astype(jnp.bfloat16)
    grad_out = jnp.einsum(
        "ti,to->io", context_low, grad_attention, preferred_element_type=jnp.float32
    )
    grad_out_bias = column_sums(grad_attention)
    grad_context = jnp.einsum(
        "to,io->ti", grad_attention, out_again, preferred_element_type=jnp.float32
    )
    grad_context = grad_context.astype(jnp.bfloat16).reshape(tiled)
    grad_values = jnp.einsum(
        "rnhqk,rnqhe->rnkhe", probs_low, grad_context, preferred_element_type=jnp.float32
    )
    grad_probs = jnp.einsum(
        "rnqhe,rnkhe->rnhqk", grad_context, value_heads, preferred_element_type=jnp.float32
    )
    probs = jnp.exp(masked_scores() - log_total)
    grad_scores = (
        probs * (grad_probs - jnp.sum(probs * grad_probs, axis=-1, keepdims=True))
    ).astype(jnp.bfloat16)
    grad_queries = (
        jnp.einsum("rnhqk,rnkhe->rnqhe", grad_scores, key_heads, preferred_element_type=jnp.float32)
        * scaling
    )
    grad_keys = (
        jnp.einsum("rnhqk,rnqhe->rnkhe", grad_scores, queries, preferred_element_type=jnp.float32)
        * scaling
    )
    grad_qkv = jnp.concatenate(
        [
            grad_queries.reshape(tokens, model_width),
            grad_keys.reshape(tokens, model_width),
            grad_values.reshape(tokens, model_width),
        ],
        axis=1,
    ).astype(jnp.bfloat16)
    grad_qkv_weight = jnp.einsum("td,te->de", first, grad_qkv, preferred_element_type=jnp.float32)
    grad_query_bias = column_sums(grad_qkv[:, :model_width])
    grad_value_bias = column_sums(grad_qkv[:, 2 * model_width :])
    grad_first = jnp.einsum("te,de->td", grad_qkv, qkv_again, preferred_element_type=jnp.float32)
    grad_in_norm, grad_gain_one, grad_shift_one = norm_back_one(grad_first)
    grad_inputs = (
        (grad_middle + grad_in_norm)
        .astype(jnp.bfloat16)
        .reshape(row_count, slot_count, model_width)
    )
    attn_total = reduce_blocks([blocks(grad_qkv_weight), blocks(grad_out)], count)
    rows = [
        grad_gain_one, grad_shift_one, grad_query_bias, grad_value_bias, grad_out_bias,
        grad_gain_two, grad_shift_two, grad_down_bias,
    ]
    sums = sum_all(
        jnp.concatenate([jnp.stack(rows), grad_up_bias.reshape(-1, model_width)]), count
    )
    share = model_width // count
    mine = lax.dynamic_slice_in_dim(sums[:8], lax.axis_index(AXIS) * share, share, axis=1)
    wider = b_up.shape[0]
    up_share = lax.dynamic_slice_in_dim(
        sums[8:].reshape(-1), lax.axis_index(AXIS) * wider, wider
    )
    return (
        result,
        grad_inputs,
        mine[0],
        mine[1],
        attn_total[:, : 3 * model_width],
        mine[2],
        mine[3],
        attn_total[:, 3 * model_width :],
        mine[4],
        mine[5],
        mine[6],
        up_total,
        up_share,
        down_total,
        mine[7],
    )


def solution(mesh):
    return jax.shard_map(
        shards,
        mesh=mesh,
        in_specs=(
            P("fsdp", None, None),
            P("fsdp", None),
            P("fsdp", None, None),
            P("fsdp"),
            P("fsdp"),
            P("fsdp", None),
            P("fsdp"),
            P("fsdp"),
            P("fsdp", None),
            P("fsdp"),
            P("fsdp"),
            P("fsdp"),
            P("fsdp", None),
            P("fsdp"),
            P("fsdp", None),
            P("fsdp"),
        ),
        out_specs=(
            P("fsdp", None, None),
            P("fsdp", None, None),
            P("fsdp"),
            P("fsdp"),
            P("fsdp", None),
            P("fsdp"),
            P("fsdp"),
            P("fsdp", None),
            P("fsdp"),
            P("fsdp"),
            P("fsdp"),
            P("fsdp", None),
            P("fsdp"),
            P("fsdp", None),
            P("fsdp"),
        ),
        check_vma=False,
    )
```

```python
import jax
import jax.numpy as jnp
from jax import lax
from jax.experimental import pallas as pl
from jax.experimental.pallas import tpu as pltpu
from jax.sharding import PartitionSpec as P

HEAD_DIM = 64
PAIR = 2 * HEAD_DIM
LANES = 128
EPSILON = 1e-06
BLOCKED = -1e9
AXIS = "fsdp"
FF_TILE = 384
VMEM_LIMIT = 60 << 20
F32 = jnp.float32
BF16 = jnp.bfloat16


def wide(value):
    return value.astype(F32)


def low(value):
    return value.astype(BF16)


def dot(left, right, left_dim=1, right_dim=0):
    return lax.dot_general(
        left, right, (((left_dim,), (right_dim,)), ((), ())), preferred_element_type=F32
    )


def split_bits(count):
    bits = count.bit_length() - 1
    plane = min(bits - 1, 2) if bits <= 5 else min(bits - 1, 4)
    return 1 << plane, 1 << (bits - 1 - plane), plane + 1


def swap(value, mask, count):
    return lax.ppermute(value, AXIS, [(i, i ^ mask) for i in range(count)])


def my_id():
    return lax.axis_index(AXIS).astype(jnp.int32)[None]


def gather_column(shard, count):
    _, depth, zbit = split_bits(count)
    own = shard[None]
    return jnp.concatenate([own] + [swap(own, m << zbit, count) for m in range(1, depth)], axis=0)


def gather_plane(column, count):
    planes, _, _ = split_bits(count)
    return [column] + [swap(column, q << 1, count) for q in range(1, planes)]


def gather_core(plane, count):
    return plane + [swap(piece, 1, count) for piece in plane]


def lay_out(pieces, count):
    planes, depth, zbit = split_bits(count)
    block = pieces[0].shape[1:]

    def body(id_ref, *refs):
        sources, out, sems = refs[: len(pieces)], refs[-2], refs[-1]
        copies = []
        for index, source in enumerate(sources):
            c, q = index // planes, index % planes
            for m in range(depth):
                target = id_ref[0] ^ (c | q << 1 | m << zbit)
                copy = pltpu.make_async_copy(
                    source.at[m], out.at[target], sems.at[index * depth + m]
                )
                copy.start()
                copies.append(copy)
        for copy in copies:
            copy.wait()

    full = pl.pallas_call(
        body,
        out_shape=jax.ShapeDtypeStruct((count,) + block, pieces[0].dtype),
        in_specs=[pl.BlockSpec(memory_space=pltpu.SMEM)]
        + [pl.BlockSpec(memory_space=pl.ANY)] * len(pieces),
        out_specs=pl.BlockSpec(memory_space=pltpu.VMEM),
        scratch_shapes=[pltpu.SemaphoreType.DMA((count,))],
        name="lay_out",
    )(my_id(), *pieces)
    return full.reshape((count * block[0],) + block[1:])


def reduce_core(keep, send, count):
    planes, depth, _ = split_bits(count)
    shape = (depth, planes) + keep.shape[1:]
    mine, other = keep.reshape(shape), swap(send, 1, count).reshape(shape)
    return [low(wide(mine[:, q]) + wide(other[:, q])) for q in range(planes)]


def reduce_plane(parts, count):
    total = wide(parts[0])
    for q in range(1, len(parts)):
        total = total + wide(swap(parts[q], q << 1, count))
    return low(total)


def reduce_column(column, count):
    _, depth, zbit = split_bits(count)
    total = wide(column[0])
    for m in range(1, depth):
        total = total + wide(swap(column[m], m << zbit, count))
    return total


def same(rows, columns, shift, period):
    row = lax.broadcasted_iota(jnp.int32, (rows, columns), 0)
    column = lax.broadcasted_iota(jnp.int32, (rows, columns), 1)
    return row == shift + column % period


def owned(count, columns, share):
    row = lax.broadcasted_iota(jnp.int32, (count, columns), 0)
    column = lax.broadcasted_iota(jnp.int32, (count, columns), 1)
    return row == column // share


def pack_small(vectors, rows):
    flat = jnp.concatenate([low(vector) for vector in vectors])
    used = -(-flat.shape[0] // LANES)
    flat = jnp.pad(flat, (0, used * LANES - flat.shape[0])).reshape(used, LANES)
    return jnp.pad(flat, ((0, rows - used), (0, 0)))


def unpack_small(weights, count, width, wider):
    rows = width // count
    share, long_share = rows, wider // count
    used = -(-(8 * share + long_share) // LANES)

    def body(block_ref, vectors_ref, long_ref):
        block = wide(block_ref[...]).reshape(count, rows, LANES)
        flat = [low(block[:, line, :]) for line in range(used)]

        def spread(shift, period, columns):
            total = jnp.zeros((count, columns), F32)
            for line in range(used):
                pick = same(LANES, columns, shift - line * LANES, period)
                total = total + dot(flat[line], low(pick.astype(F32)))
            mine = jnp.where(owned(count, columns, period), total, 0.0)
            return jnp.sum(mine, axis=0, keepdims=True)

        for v in range(8):
            vectors_ref[v : v + 1, :] = spread(v * share, share, width)
        long_ref[...] = spread(8 * share, long_share, wider)

    return pl.pallas_call(
        body,
        grid=(1,),
        out_shape=(jax.ShapeDtypeStruct((8, width), F32), jax.ShapeDtypeStruct((1, wider), F32)),
        in_specs=[pl.BlockSpec((width, LANES), lambda i: (0, weights.shape[1] // LANES - 1))],
        out_specs=(
            pl.BlockSpec((8, width), lambda i: (0, 0)),
            pl.BlockSpec((1, wider), lambda i: (0, 0)),
        ),
        name="unpack_small",
    )(weights)


def normalized(value):
    centred = value - jnp.mean(value, axis=-1, keepdims=True)
    scale = lax.rsqrt(jnp.mean(centred * centred, axis=-1, keepdims=True) + EPSILON)
    return centred * scale, scale


def norm_back(grad, unit, scale, gain):
    inner = grad * gain
    average = jnp.mean(inner, axis=-1, keepdims=True)
    along = jnp.mean(inner * unit, axis=-1, keepdims=True)
    return scale * (inner - average - unit * along)


def column_sums(value):
    return jnp.sum(value, axis=0, keepdims=True)


def halves():
    lane = lax.broadcasted_iota(jnp.int32, (1, PAIR), 1)
    first = low((lane < HEAD_DIM).astype(F32))
    return first, low((lane >= HEAD_DIM).astype(F32))


def mask_of(across, down):
    slots = across.shape[1]
    row = lax.broadcasted_iota(jnp.int32, (slots, slots), 0)
    column = lax.broadcasted_iota(jnp.int32, (slots, slots), 1)
    allowed = ((down == across) & (down > 0)) | (row == column)
    return jnp.where(allowed, 0.0, BLOCKED)


def spread(product, rows, count, me, keep, send):
    for couple in range(count // 2):
        slot = couple ^ (me // 2)
        even = low(product[2 * couple * rows : (2 * couple + 1) * rows, :])
        odd = low(product[(2 * couple + 1) * rows : (2 * couple + 2) * rows, :])
        keep[slot] = jnp.where(me % 2 == 0, even, odd)
        send[slot] = jnp.where(me % 2 == 0, odd, even)


def attend(x, across, down, weights, vectors):
    tokens, width = x.shape
    slots = across.shape[2]
    rows = tokens // slots
    heads = width // HEAD_DIM

    def body(x_ref, across_ref, down_ref, w_ref, vec_ref, first_ref, qkv_ref, ctx_ref, lse_ref, mid_ref, second_ref):
        value = wide(x_ref[...])
        unit, _ = normalized(value)
        first = low(unit * vec_ref[0:1, :] + vec_ref[1:2, :])
        first_ref[...] = first
        for part in range(3):
            product = dot(first, w_ref[:, part * width : (part + 1) * width])
            if part != 1:
                product = product + vec_ref[2 + part // 2 : 3 + part // 2, :]
            qkv_ref[:, part * width : (part + 1) * width] = low(product)
        bias = mask_of(across_ref[0], down_ref[...])
        masks = halves()
        for pair in range(heads // 2):
            lanes = slice(pair * PAIR, (pair + 1) * PAIR)
            q = qkv_ref[:, lanes]
            k = qkv_ref[:, width + pair * PAIR : width + (pair + 1) * PAIR]
            v = qkv_ref[:, 2 * width + pair * PAIR : 2 * width + (pair + 1) * PAIR]
            context = jnp.zeros((slots, PAIR), F32)
            for side in range(2):
                scores = dot(q * masks[side], k, 1, 1) * HEAD_DIM**-0.5 + bias
                highest = jnp.max(scores, axis=-1, keepdims=True)
                powers = jnp.exp(scores - highest)
                total = jnp.sum(powers, axis=-1, keepdims=True)
                probs = low(powers * (1.0 / total))
                context = context + dot(probs, v * masks[side])
                head = 2 * pair + side
                lse_ref[:, head : head + 1] = highest + jnp.log(total)
            ctx_ref[:, lanes] = low(context)
        attention = dot(ctx_ref[...], w_ref[:, 3 * width : 4 * width]) + vec_ref[4:5, :]
        middle = value + attention
        mid_ref[...] = middle
        unit, _ = normalized(middle)
        second_ref[...] = low(unit * vec_ref[5:6, :] + vec_ref[6:7, :])

    def row(columns):
        return pl.BlockSpec((slots, columns), lambda i: (i, 0))

    def whole(array):
        return pl.BlockSpec(array.shape, lambda i: (0, 0), pipeline_mode=pl.Buffered(1))

    shapes = [(width, BF16), (3 * width, BF16), (width, BF16), (heads, F32), (width, F32), (width, BF16)]
    return pl.pallas_call(
        body,
        grid=(rows,),
        out_shape=tuple(jax.ShapeDtypeStruct((tokens, c), t) for c, t in shapes),
        in_specs=[
            row(width),
            pl.BlockSpec((1, 1, slots), lambda i: (i, 0, 0)),
            row(1),
            whole(weights),
            whole(vectors),
        ],
        out_specs=tuple(row(c) for c, _ in shapes),
        compiler_params=pltpu.CompilerParams(vmem_limit_bytes=VMEM_LIMIT),
        cost_estimate=pl.CostEstimate(
            flops=2 * tokens * width * width * 4 + 4 * rows * heads * slots * slots * HEAD_DIM,
            transcendentals=rows * heads * slots * slots,
            bytes_accessed=30 << 20,
        ),
        name="attend",
    )(x, across, down, weights, vectors)


def feed_forward(second, upstream, middle, up, down, vectors, long_bias, count):
    tokens, width = second.shape
    wider = up.shape[1]
    tile = FF_TILE
    steps = wider // tile
    up_rows, down_rows = width // count, wider // count
    group = tile // down_rows

    def body(
        id_ref, second_ref, grad_ref, mid_ref, up_ref, down_ref, vec_ref, bias_ref,
        out_ref, dmid_ref, up_keep, up_send, down_keep, down_send, long_ref, rows_ref,
        out_sum, back_sum, second_turned, up_product, down_product,
    ):
        step = pl.program_id(0)
        me = id_ref[0]

        @pl.when(step == 0)
        def _():
            second_turned[...] = second_ref[...].T
            out_sum[...] = jnp.zeros_like(out_sum)
            back_sum[...] = jnp.zeros_like(back_sum)

        grads = grad_ref[...]
        hidden = dot(second_ref[...], up_ref[...]) + bias_ref[...]
        below = 0.5 * (1.0 + lax.erf(hidden * 0.7071067811865476))
        active = low(hidden * below)
        slope = below + hidden * (jnp.exp(hidden * hidden * -0.5) * 0.3989422804014327)
        back = dot(grads, down_ref[...], 1, 1) * slope
        back_low = low(back)
        long_ref[...] = column_sums(wide(back_low))
        out_sum[...] += dot(active, down_ref[...])
        back_sum[...] += dot(back_low, up_ref[...], 1, 1)
        up_product[...] = dot(second_turned[...], back_low)
        down_product[...] = dot(active, grads, 0, 0)

        spread(up_product, up_rows, count, me, up_keep, up_send)
        spread(down_product, down_rows, group, me % group, down_keep, down_send)

        @pl.when(step == steps - 1)
        def _():
            middle_now = mid_ref[...]
            out_ref[...] = low(middle_now + (out_sum[...] + vec_ref[7:8, :]))
            unit, scale = normalized(middle_now)
            da = back_sum[...]
            dmid_ref[...] = wide(grads) + norm_back(da, unit, scale, vec_ref[5:6, :])
            rows_ref[0:1, :] = column_sums(da * unit)
            rows_ref[1:2, :] = column_sums(da)
            rows_ref[2:3, :] = column_sums(wide(grads))

    def whole(array):
        return pl.BlockSpec(array.shape, lambda i, m: (0, 0), pipeline_mode=pl.Buffered(1))

    def fixed(shape):
        return pl.BlockSpec(shape, lambda i, m: (0,) * len(shape))

    half = count // 2
    up_spec = pl.BlockSpec((half, up_rows, tile), lambda i, m: (0, 0, i))
    down_spec = pl.BlockSpec((group // 2, down_rows, width), lambda i, m: (i ^ (m[0] // group), 0, 0))
    return pl.pallas_call(
        body,
        grid_spec=pltpu.PrefetchScalarGridSpec(
            num_scalar_prefetch=1,
            grid=(steps,),
            in_specs=[
                whole(second), whole(upstream), whole(middle),
                pl.BlockSpec((width, tile), lambda i, m: (0, i)),
                pl.BlockSpec((tile, width), lambda i, m: (i, 0)),
                whole(vectors),
                pl.BlockSpec((1, tile), lambda i, m: (0, i)),
            ],
            out_specs=(
                fixed((tokens, width)), fixed((tokens, width)),
                up_spec, up_spec, down_spec, down_spec,
                pl.BlockSpec((1, tile), lambda i, m: (0, i)),
                fixed((8, width)),
            ),
            scratch_shapes=[
                pltpu.VMEM((tokens, width), F32), pltpu.VMEM((tokens, width), F32),
                pltpu.VMEM((width, tokens), BF16),
                pltpu.VMEM((width, tile), F32), pltpu.VMEM((tile, width), F32),
            ],
        ),
        out_shape=(
            jax.ShapeDtypeStruct((tokens, width), BF16),
            jax.ShapeDtypeStruct((tokens, width), F32),
            jax.ShapeDtypeStruct((half, up_rows, wider), BF16),
            jax.ShapeDtypeStruct((half, up_rows, wider), BF16),
            jax.ShapeDtypeStruct((half, down_rows, width), BF16),
            jax.ShapeDtypeStruct((half, down_rows, width), BF16),
            jax.ShapeDtypeStruct((1, wider), F32),
            jax.ShapeDtypeStruct((8, width), F32),
        ),
        compiler_params=pltpu.CompilerParams(vmem_limit_bytes=VMEM_LIMIT),
        cost_estimate=pl.CostEstimate(
            flops=12 * tokens * width * wider, transcendentals=2 * tokens * wider,
            bytes_accessed=35 << 20,
        ),
        name="feed_forward",
    )(my_id(), second, upstream, middle, up, down, vectors, long_bias)


def attend_back(x, across, down, weights, vectors, first, qkv, context, lse, dmid, mlp_rows, long_row, count):
    tokens, width = x.shape
    slots = across.shape[2]
    rows = tokens // slots
    heads = width // HEAD_DIM
    wider = long_row.shape[1]
    share, long_share = width // count, wider // count
    used = -(-(8 * share + long_share) // LANES)

    def body(
        id_ref, x_ref, across_ref, down_ref, w_ref, vec_ref, first_ref, qkv_ref, ctx_ref, lse_ref,
        dmid_ref, mlp_ref, long_ref,
        dx_ref, keep_ref, send_ref,
        dqkv_all, dattn_all, product, sums, dctx,
    ):
        step = pl.program_id(0)
        me = id_ref[0]

        @pl.when(step == 0)
        def _():
            sums[...] = jnp.zeros_like(sums)

        here = pl.ds(pl.multiple_of(step * slots, slots), slots)
        middle_grad = dmid_ref[...]
        dattn = low(middle_grad)
        dattn_all[here, :] = dattn
        dctx[...] = low(dot(dattn, w_ref[:, 3 * width : 4 * width], 1, 1))
        bias = mask_of(across_ref[0], down_ref[...])
        masks = halves()
        for pair in range(heads // 2):
            lanes = [slice(p * width + pair * PAIR, p * width + (pair + 1) * PAIR) for p in range(3)]
            mine = pl.ds(pl.multiple_of(step * slots, slots), slots)
            q, k, v = (qkv_ref[mine, lane] for lane in lanes)
            dout = dctx[:, lanes[0]]
            dq = jnp.zeros((slots, PAIR), F32)
            dk = jnp.zeros((slots, PAIR), F32)
            dv = jnp.zeros((slots, PAIR), F32)
            for side in range(2):
                head = 2 * pair + side
                q_half, dout_half = q * masks[side], dout * masks[side]
                scores = dot(q_half, k, 1, 1) * HEAD_DIM**-0.5 + bias
                probs = jnp.exp(scores - lse_ref[:, head : head + 1])
                dprobs = dot(dout_half, v, 1, 1)
                weighted = probs * dprobs
                dscores = low(weighted - probs * jnp.sum(weighted, axis=-1, keepdims=True))
                dv = dv + dot(low(probs), dout_half, 0, 0)
                dq = dq + dot(dscores, k * masks[side])
                dk = dk + dot(dscores, q_half, 0, 0)
            dqkv_all[here, lanes[0]] = low(dq * HEAD_DIM**-0.5)
            dqkv_all[here, lanes[1]] = low(dk * HEAD_DIM**-0.5)
            dqkv_all[here, lanes[2]] = low(dv)
        dfirst = jnp.zeros((slots, width), F32)
        for p in range(3):
            part = slice(p * width, (p + 1) * width)
            dfirst = dfirst + dot(dqkv_all[here, part], w_ref[:, part], 1, 1)
        unit, scale = normalized(wide(x_ref[...]))
        dx_ref[...] = low(middle_grad + norm_back(dfirst, unit, scale, vec_ref[0:1, :]))
        sums[0:1, :] += column_sums(dfirst * unit)
        sums[1:2, :] += column_sums(dfirst)
        sums[2:3, :] += column_sums(wide(dqkv_all[here, :width]))
        sums[3:4, :] += column_sums(wide(dqkv_all[here, 2 * width :]))
        sums[4:5, :] += column_sums(wide(dattn))

        @pl.when(step == rows - 1)
        def _():
            for p in range(4):
                part = slice(p * width, (p + 1) * width)
                if p < 3:
                    product[...] = dot(first_ref[...], dqkv_all[:, part], 0, 0)
                else:
                    product[...] = dot(ctx_ref[...], dattn_all[...], 0, 0)

                spread(
                    product, share, count, me, keep_ref.at[:, :, part], send_ref.at[:, :, part]
                )

            def fold(row, shift, period):
                columns = row.shape[1]
                mine = low(jnp.where(owned(count, columns, period), row, 0.0))
                found = []
                for line in range(used):
                    pick = same(LANES, columns, shift - line * LANES, period)
                    found.append(dot(mine, low(pick.astype(F32)), 1, 1))
                return found

            lines = fold(long_ref[...], 8 * share, long_share)
            for v in range(8):
                row = sums[v : v + 1, :] if v < 5 else mlp_ref[v - 5 : v - 4, :]
                lines = [old + new for old, new in zip(lines, fold(row, v * share, share))]
            number = lax.broadcasted_iota(jnp.int32, (share, LANES), 0)

            def block_of(owner):
                block = jnp.zeros((share, LANES), F32)
                for line in range(used):
                    block = jnp.where(number == line, lines[line][owner : owner + 1, :], block)
                return low(block)

            for couple in range(count // 2):
                slot = couple ^ (me // 2)
                even, odd = block_of(2 * couple), block_of(2 * couple + 1)
                keep_ref[slot, :, 4 * width :] = jnp.where(me % 2 == 0, even, odd)
                send_ref[slot, :, 4 * width :] = jnp.where(me % 2 == 0, odd, even)

    def row(columns):
        return pl.BlockSpec((slots, columns), lambda i, m: (i, 0))

    def whole(array):
        return pl.BlockSpec(array.shape, lambda i, m: (0, 0), pipeline_mode=pl.Buffered(1))

    block = (count // 2, share, 4 * width + LANES)
    block_spec = pl.BlockSpec(block, lambda i, m: (0, 0, 0), pipeline_mode=pl.Buffered(1))
    return pl.pallas_call(
        body,
        grid_spec=pltpu.PrefetchScalarGridSpec(
            num_scalar_prefetch=1,
            grid=(rows,),
            in_specs=[
                row(width),
                pl.BlockSpec((1, 1, slots), lambda i, m: (i, 0, 0)),
                row(1), whole(weights), whole(vectors), whole(first), whole(qkv), whole(context),
                row(heads), row(width), whole(mlp_rows), whole(long_row),
            ],
            out_specs=(row(width), block_spec, block_spec),
            scratch_shapes=[
                pltpu.VMEM((tokens, 3 * width), BF16), pltpu.VMEM((tokens, width), BF16),
                pltpu.VMEM((width, width), F32), pltpu.VMEM((8, width), F32),
                pltpu.VMEM((slots, width), BF16),
            ],
        ),
        out_shape=(
            jax.ShapeDtypeStruct((tokens, width), BF16),
            jax.ShapeDtypeStruct(block, BF16), jax.ShapeDtypeStruct(block, BF16),
        ),
        compiler_params=pltpu.CompilerParams(vmem_limit_bytes=VMEM_LIMIT),
        cost_estimate=pl.CostEstimate(
            flops=2 * tokens * width * width * 8 + 10 * rows * heads * slots * slots * HEAD_DIM,
            transcendentals=rows * heads * slots * slots,
            bytes_accessed=35 << 20,
        ),
        name="attend_back",
    )(my_id(), x, across, down, weights, vectors, first, qkv, context, lse, dmid, mlp_rows, long_row)


def shards(
    layer_input, segments, cotangent, pre_gain, pre_shift, w_qkv, b_query, b_value, w_out, b_out,
    mid_gain, mid_shift, w_up, b_up, w_down, b_down,
):
    row_count, slot_count, width = layer_input.shape
    tokens = row_count * slot_count
    share, long_share = pre_gain.shape[0], b_up.shape[0]
    count = width // share
    small = [pre_gain, pre_shift, b_query, b_value, b_out, mid_gain, mid_shift, b_down, b_up]
    near = jnp.concatenate([low(w_qkv), low(w_out), pack_small(small, share)], axis=1)

    near_column = gather_column(near, count)
    up_column = gather_column(low(w_up), count)
    down_column = gather_column(low(w_down), count)
    near_full = lay_out(gather_core(gather_plane(near_column, count), count), count)
    up_full = lay_out(gather_core(gather_plane(up_column, count), count), count)
    down_full = lay_out(gather_core(gather_plane(down_column, count), count), count)

    x = layer_input.reshape(tokens, width)
    grads = cotangent.reshape(tokens, width)
    across = segments.reshape(row_count, 1, slot_count)
    down = segments.reshape(tokens, 1)
    vectors, long_bias = unpack_small(near_full, count, width, count * long_share)
    first, qkv, context, lse, middle, second = attend(x, across, down, near_full, vectors)
    result, dmid, up_keep, up_send, down_keep, down_send, long_row, mlp_rows = feed_forward(
        second, grads, middle, up_full, down_full, vectors, long_bias, count
    )
    up_total = reduce_column(reduce_plane(reduce_core(up_keep, up_send, count), count), count)
    down_total = reduce_column(reduce_plane(reduce_core(down_keep, down_send, count), count), count)
    dx, keep, send = attend_back(
        x, across, down, near_full, vectors, first, qkv, context, lse, dmid, mlp_rows, long_row, count
    )
    total = reduce_column(reduce_plane(reduce_core(keep, send, count), count), count)
    used = -(-(8 * share + long_share) // LANES)
    flat = total[:used, 4 * width :].reshape(-1)
    vector_grads = [flat[v * share : (v + 1) * share] for v in range(8)]
    return (
        result.reshape(layer_input.shape),
        dx.reshape(layer_input.shape),
        vector_grads[0],
        vector_grads[1],
        total[:, : 3 * width],
        vector_grads[2],
        vector_grads[3],
        total[:, 3 * width : 4 * width],
        vector_grads[4],
        vector_grads[5],
        vector_grads[6],
        up_total,
        flat[8 * share : 8 * share + long_share],
        down_total,
        vector_grads[7],
    )


def solution(mesh):
    line, table = P(AXIS), P(AXIS, None)
    cube = P(AXIS, None, None)
    return jax.shard_map(
        shards,
        mesh=mesh,
        in_specs=(
            cube, table, cube, line, line, table, line, line, table, line, line, line, table, line,
            table, line,
        ),
        out_specs=(
            cube, cube, line, line, table, line, line, table, line, line, line, table, line, table,
            line,
        ),
        check_vma=False,
    )
```

```python
import jax
import jax.numpy as jnp
from jax import lax
from jax.experimental import pallas as pl
from jax.experimental.pallas import tpu as pltpu
from jax.sharding import PartitionSpec as P

HEAD_DIM = 64
PAIR = 2 * HEAD_DIM
LANES = 128
EPSILON = 1e-06
BLOCKED = -1e9
AXIS = "fsdp"
FF_TILE = 384
VMEM_LIMIT = 60 << 20
F32 = jnp.float32
BF16 = jnp.bfloat16


def wide(value):
    return value.astype(F32)


def low(value):
    return value.astype(BF16)


def dot(left, right, left_dim=1, right_dim=0):
    return lax.dot_general(
        left, right, (((left_dim,), (right_dim,)), ((), ())), preferred_element_type=F32
    )


def axes_of(count):
    rest = count.bit_length() - 2
    side = rest // 3
    return (1 << side, 1), (1 << side, 1 + side), (1 << (rest - 2 * side), 1 + 2 * side)


def swap(value, mask, count):
    return lax.ppermute(value, AXIS, [(i, i ^ mask) for i in range(count)])


def my_id():
    return lax.axis_index(AXIS).astype(jnp.int32)[None]


def gather(value, axis, count):
    size, bit = axis
    return [value] + [swap(value, d << bit, count) for d in range(1, size)]


def gather_chips(shard, count):
    x, y, z = axes_of(count)
    column = jnp.stack(gather(shard, z, count))
    half = z[0] // 2
    left = jnp.stack(gather(column[:half], x, count))
    right = jnp.stack(gather(column[half:], y, count))
    return gather(left, y, count) + gather(right, x, count)


def gather_core(pieces, count):
    return pieces + [swap(piece, 1, count) for piece in pieces]


def lay_out(pieces, count):
    (xs, xbit), (ys, ybit), (zs, zbit) = axes_of(count)
    block = pieces[0].shape[2:]
    half = zs // 2

    def body(id_ref, *refs):
        sources, out, sems = refs[: len(pieces)], refs[-2], refs[-1]
        copies = []
        for index, source in enumerate(sources):
            c, place = divmod(index, ys + xs)
            for inner in range(source.shape[0]):
                for m in range(half):
                    if place < ys:
                        block_id = c | inner << xbit | place << ybit | m << zbit
                    else:
                        block_id = c | (place - ys) << xbit | inner << ybit | (m + half) << zbit
                    copy = pltpu.make_async_copy(
                        source.at[inner, m], out.at[id_ref[0] ^ block_id], sems.at[len(copies)]
                    )
                    copy.start()
                    copies.append(copy)
        for copy in copies:
            copy.wait()

    full = pl.pallas_call(
        body,
        out_shape=jax.ShapeDtypeStruct((count,) + block, pieces[0].dtype),
        in_specs=[pl.BlockSpec(memory_space=pltpu.SMEM)]
        + [pl.BlockSpec(memory_space=pl.ANY)] * len(pieces),
        out_specs=pl.BlockSpec(memory_space=pltpu.VMEM),
        scratch_shapes=[pltpu.SemaphoreType.DMA((count,))],
        name="lay_out",
    )(my_id(), *pieces)
    return full.reshape((count * block[0],) + block[1:])


def reduce_axis(parts, axis, count):
    size, bit = axis
    total = wide(parts[0])
    for d in range(1, size):
        total = total + wide(swap(parts[d], d << bit, count))
    return total


def reduce_blocks(keep, send, count):
    x, y, z = axes_of(count)
    shape = (z[0], y[0], x[0]) + keep.shape[1:]
    both = wide(keep) + wide(swap(send, 1, count))
    both = low(both).reshape(shape)
    half = z[0] // 2
    left = [both[:half, :, d] for d in range(x[0])]
    left = low(reduce_axis(left, x, count))
    right = [both[half:, d] for d in range(y[0])]
    right = low(reduce_axis(right, y, count))
    left = low(reduce_axis([left[:, d] for d in range(y[0])], y, count))
    right = low(reduce_axis([right[:, d] for d in range(x[0])], x, count))
    column = [left[m] for m in range(half)] + [right[m] for m in range(half)]
    return reduce_axis(column, z, count)


def same(rows, columns, shift, period):
    row = lax.broadcasted_iota(jnp.int32, (rows, columns), 0)
    column = lax.broadcasted_iota(jnp.int32, (rows, columns), 1)
    return row == shift + column % period


def owned(count, columns, share):
    row = lax.broadcasted_iota(jnp.int32, (count, columns), 0)
    column = lax.broadcasted_iota(jnp.int32, (count, columns), 1)
    return row == column // share


def pack_near(qkv, out, vectors):
    rows = qkv.shape[0]
    sizes = [vector.shape[0] for vector in vectors]
    used = -(-sum(sizes) // LANES)
    columns = qkv.shape[1] + out.shape[1] + LANES

    def body(qkv_ref, out_ref, *refs):
        near_ref = refs[-1]
        near_ref[:, : qkv.shape[1]] = low(qkv_ref[...])
        near_ref[:, qkv.shape[1] : columns - LANES] = low(out_ref[...])
        number = lax.broadcasted_iota(jnp.int32, (rows, LANES), 0)
        block = jnp.zeros((rows, LANES), F32)
        for line in range(used):
            text, start = jnp.zeros((8, LANES), F32), 0
            for ref, size in zip(refs, sizes):
                if start < (line + 1) * LANES and start + size > line * LANES:
                    column = lax.broadcasted_iota(jnp.int32, (size, LANES), 1)
                    row = lax.broadcasted_iota(jnp.int32, (size, LANES), 0)
                    pick = low((column == row + (start - line * LANES)).astype(F32))
                    text = text + dot(low(jnp.broadcast_to(ref[...], (8, size))), pick)
                start += size
            block = jnp.where(number == line, text[:1], block)
        near_ref[:, columns - LANES :] = low(block)

    vmem = pl.BlockSpec(memory_space=pltpu.VMEM)
    return pl.pallas_call(
        body,
        out_shape=jax.ShapeDtypeStruct((rows, columns), BF16),
        in_specs=[vmem] * (2 + len(vectors)),
        out_specs=vmem,
        name="pack_near",
    )(qkv, out, *[vector.reshape(1, -1) for vector in vectors])


def unpack_small(weights, count, width, wider):
    rows = width // count
    share, long_share = rows, wider // count
    used = -(-(8 * share + long_share) // LANES)

    def body(block_ref, vectors_ref, long_ref):
        block = wide(block_ref[...]).reshape(count, rows, LANES)
        flat = [low(block[:, line, :]) for line in range(used)]

        def spread(shift, period, columns):
            total = jnp.zeros((count, columns), F32)
            for line in range(used):
                pick = same(LANES, columns, shift - line * LANES, period)
                total = total + dot(flat[line], low(pick.astype(F32)))
            mine = jnp.where(owned(count, columns, period), total, 0.0)
            return jnp.sum(mine, axis=0, keepdims=True)

        for v in range(8):
            vectors_ref[v : v + 1, :] = spread(v * share, share, width)
        long_ref[...] = spread(8 * share, long_share, wider)

    return pl.pallas_call(
        body,
        grid=(1,),
        out_shape=(jax.ShapeDtypeStruct((8, width), F32), jax.ShapeDtypeStruct((1, wider), F32)),
        in_specs=[pl.BlockSpec((width, LANES), lambda i: (0, weights.shape[1] // LANES - 1))],
        out_specs=(
            pl.BlockSpec((8, width), lambda i: (0, 0)),
            pl.BlockSpec((1, wider), lambda i: (0, 0)),
        ),
        name="unpack_small",
    )(weights)


def normalized(value):
    centred = value - jnp.mean(value, axis=-1, keepdims=True)
    scale = lax.rsqrt(jnp.mean(centred * centred, axis=-1, keepdims=True) + EPSILON)
    return centred * scale, scale


def norm_back(grad, unit, scale, gain):
    inner = grad * gain
    average = jnp.mean(inner, axis=-1, keepdims=True)
    along = jnp.mean(inner * unit, axis=-1, keepdims=True)
    return scale * (inner - average - unit * along)


def column_sums(value):
    return jnp.sum(value, axis=0, keepdims=True)


def halves():
    lane = lax.broadcasted_iota(jnp.int32, (1, PAIR), 1)
    first = low((lane < HEAD_DIM).astype(F32))
    return first, low((lane >= HEAD_DIM).astype(F32))


def mask_of(across, down):
    slots = across.shape[1]
    row = lax.broadcasted_iota(jnp.int32, (slots, slots), 0)
    column = lax.broadcasted_iota(jnp.int32, (slots, slots), 1)
    allowed = ((down == across) & (down > 0)) | (row == column)
    return jnp.where(allowed, 0.0, BLOCKED)


def spread(product, rows, count, me, keep, send):
    if rows % 8 == 0:

        def place(slot, carry):
            for c, out in enumerate((keep, send)):
                start = pl.multiple_of((me ^ (2 * slot + c)) * rows, 8)
                out[slot] = low(product[pl.ds(start, rows), :])
            return carry

        lax.fori_loop(0, count // 2, place, 0)
        return
    for couple in range(count // 2):
        slot = couple ^ (me // 2)
        even = low(product[2 * couple * rows : (2 * couple + 1) * rows, :])
        odd = low(product[(2 * couple + 1) * rows : (2 * couple + 2) * rows, :])
        keep[slot] = jnp.where(me % 2 == 0, even, odd)
        send[slot] = jnp.where(me % 2 == 0, odd, even)


def attend(x, across, down, weights, vectors):
    tokens, width = x.shape
    slots = across.shape[2]
    rows = tokens // slots
    heads = width // HEAD_DIM

    def body(x_ref, across_ref, down_ref, w_ref, vec_ref, first_ref, qkv_ref, ctx_ref, lse_ref, mid_ref, second_ref):
        value = wide(x_ref[...])
        unit, _ = normalized(value)
        first = low(unit * vec_ref[0:1, :] + vec_ref[1:2, :])
        first_ref[...] = first
        for part in range(3):
            product = dot(first, w_ref[:, part * width : (part + 1) * width])
            if part != 1:
                product = product + vec_ref[2 + part // 2 : 3 + part // 2, :]
            qkv_ref[:, part * width : (part + 1) * width] = low(product)
        bias = mask_of(across_ref[0], down_ref[...])
        masks = halves()
        for pair in range(heads // 2):
            lanes = slice(pair * PAIR, (pair + 1) * PAIR)
            q = qkv_ref[:, lanes]
            k = qkv_ref[:, width + pair * PAIR : width + (pair + 1) * PAIR]
            v = qkv_ref[:, 2 * width + pair * PAIR : 2 * width + (pair + 1) * PAIR]
            context = jnp.zeros((slots, PAIR), F32)
            for side in range(2):
                scores = dot(q * masks[side], k, 1, 1) * HEAD_DIM**-0.5 + bias
                highest = jnp.max(scores, axis=-1, keepdims=True)
                powers = jnp.exp(scores - highest)
                total = jnp.sum(powers, axis=-1, keepdims=True)
                probs = low(powers * (1.0 / total))
                context = context + dot(probs, v * masks[side])
                head = 2 * pair + side
                lse_ref[:, head : head + 1] = highest + jnp.log(total)
            ctx_ref[:, lanes] = low(context)
        attention = dot(ctx_ref[...], w_ref[:, 3 * width : 4 * width]) + vec_ref[4:5, :]
        middle = value + attention
        mid_ref[...] = middle
        unit, _ = normalized(middle)
        second_ref[...] = low(unit * vec_ref[5:6, :] + vec_ref[6:7, :])

    def row(columns):
        return pl.BlockSpec((slots, columns), lambda i: (i, 0))

    def whole(array):
        return pl.BlockSpec(array.shape, lambda i: (0, 0), pipeline_mode=pl.Buffered(1))

    shapes = [(width, BF16), (3 * width, BF16), (width, BF16), (heads, F32), (width, F32), (width, BF16)]
    return pl.pallas_call(
        body,
        grid=(rows,),
        out_shape=tuple(jax.ShapeDtypeStruct((tokens, c), t) for c, t in shapes),
        in_specs=[
            row(width),
            pl.BlockSpec((1, 1, slots), lambda i: (i, 0, 0)),
            row(1),
            whole(weights),
            whole(vectors),
        ],
        out_specs=tuple(row(c) for c, _ in shapes),
        compiler_params=pltpu.CompilerParams(vmem_limit_bytes=VMEM_LIMIT),
        cost_estimate=pl.CostEstimate(
            flops=2 * tokens * width * width * 4 + 4 * rows * heads * slots * slots * HEAD_DIM,
            transcendentals=rows * heads * slots * slots,
            bytes_accessed=30 << 20,
        ),
        name="attend",
    )(x, across, down, weights, vectors)


def feed_forward(second, upstream, middle, up, down, vectors, long_bias, count):
    tokens, width = second.shape
    wider = up.shape[1]
    tile = FF_TILE
    steps = wider // tile
    down_rows = wider // count
    group = tile // down_rows

    def body(
        id_ref, second_ref, grad_ref, mid_ref, up_ref, down_ref, vec_ref, bias_ref,
        out_ref, back_ref, down_keep, down_send, long_ref, rows_ref,
        out_sum, down_product,
    ):
        step = pl.program_id(0)
        me = id_ref[0]

        @pl.when(step == 0)
        def _():
            out_sum[...] = jnp.zeros_like(out_sum)

        grads = grad_ref[...]
        hidden = dot(second_ref[...], up_ref[...]) + bias_ref[...]
        below = 0.5 * (1.0 + lax.erf(hidden * 0.7071067811865476))
        active = low(hidden * below)
        slope = below + hidden * (jnp.exp(hidden * hidden * -0.5) * 0.3989422804014327)
        back = low(dot(grads, down_ref[...], 1, 1) * slope)
        back_ref[...] = back
        long_ref[...] = column_sums(wide(back))
        out_sum[...] += dot(active, down_ref[...])
        down_product[...] = dot(active, grads, 0, 0)
        spread(down_product, down_rows, group, me % group, down_keep, down_send)

        @pl.when(step == steps - 1)
        def _():
            out_ref[...] = low(mid_ref[...] + (out_sum[...] + vec_ref[7:8, :]))
            rows_ref[...] = jnp.broadcast_to(column_sums(wide(grads)), (8, width))

    def whole(array):
        return pl.BlockSpec(array.shape, lambda i, m: (0, 0), pipeline_mode=pl.Buffered(1))

    half = count // 2
    down_spec = pl.BlockSpec((group // 2, down_rows, width), lambda i, m: (i ^ (m[0] // group), 0, 0))
    return pl.pallas_call(
        body,
        grid_spec=pltpu.PrefetchScalarGridSpec(
            num_scalar_prefetch=1,
            grid=(steps,),
            in_specs=[
                whole(second), whole(upstream), whole(middle),
                pl.BlockSpec((width, tile), lambda i, m: (0, i)),
                pl.BlockSpec((tile, width), lambda i, m: (i, 0)),
                whole(vectors),
                pl.BlockSpec((1, tile), lambda i, m: (0, i)),
            ],
            out_specs=(
                pl.BlockSpec((tokens, width), lambda i, m: (0, 0)),
                pl.BlockSpec((tokens, tile), lambda i, m: (0, i)),
                down_spec, down_spec,
                pl.BlockSpec((1, tile), lambda i, m: (0, i)),
                pl.BlockSpec((8, width), lambda i, m: (0, 0)),
            ),
            scratch_shapes=[pltpu.VMEM((tokens, width), F32), pltpu.VMEM((tile, width), F32)],
        ),
        out_shape=(
            jax.ShapeDtypeStruct((tokens, width), BF16),
            jax.ShapeDtypeStruct((tokens, wider), BF16),
            jax.ShapeDtypeStruct((half, down_rows, width), BF16),
            jax.ShapeDtypeStruct((half, down_rows, width), BF16),
            jax.ShapeDtypeStruct((1, wider), F32),
            jax.ShapeDtypeStruct((8, width), F32),
        ),
        compiler_params=pltpu.CompilerParams(vmem_limit_bytes=VMEM_LIMIT),
        cost_estimate=pl.CostEstimate(
            flops=8 * tokens * width * wider, transcendentals=2 * tokens * wider,
            bytes_accessed=30 << 20,
        ),
        name="feed_forward",
    )(my_id(), second, upstream, middle, up, down, vectors, long_bias)


def feed_back(second, back, upstream, middle, up, vectors, count):
    tokens, width = second.shape
    wider = up.shape[1]
    tile = FF_TILE
    steps = wider // tile
    up_rows = width // count

    def body(
        id_ref, second_ref, back_ref, grad_ref, mid_ref, up_ref, vec_ref,
        dmid_ref, up_keep, up_send, rows_ref,
        back_sum, second_turned, up_product,
    ):
        step = pl.program_id(0)

        @pl.when(step == 0)
        def _():
            second_turned[...] = second_ref[...].T
            back_sum[...] = jnp.zeros_like(back_sum)

        back_sum[...] += dot(back_ref[...], up_ref[...], 1, 1)
        up_product[...] = dot(second_turned[...], back_ref[...])
        spread(up_product, up_rows, count, id_ref[0], up_keep, up_send)

        @pl.when(step == steps - 1)
        def _():
            unit, scale = normalized(mid_ref[...])
            da = back_sum[...]
            dmid_ref[...] = wide(grad_ref[...]) + norm_back(da, unit, scale, vec_ref[5:6, :])
            rows_ref[...] = jnp.zeros_like(rows_ref)
            rows_ref[0:1, :] = column_sums(da * unit)
            rows_ref[1:2, :] = column_sums(da)

    def whole(array):
        return pl.BlockSpec(array.shape, lambda i, m: (0, 0), pipeline_mode=pl.Buffered(1))

    half = count // 2
    up_spec = pl.BlockSpec((half, up_rows, tile), lambda i, m: (0, 0, i))
    return pl.pallas_call(
        body,
        grid_spec=pltpu.PrefetchScalarGridSpec(
            num_scalar_prefetch=1,
            grid=(steps,),
            in_specs=[
                whole(second),
                pl.BlockSpec((tokens, tile), lambda i, m: (0, i)),
                whole(upstream), whole(middle),
                pl.BlockSpec((width, tile), lambda i, m: (0, i)),
                whole(vectors),
            ],
            out_specs=(
                pl.BlockSpec((tokens, width), lambda i, m: (0, 0)),
                up_spec, up_spec,
                pl.BlockSpec((8, width), lambda i, m: (0, 0)),
            ),
            scratch_shapes=[
                pltpu.VMEM((tokens, width), F32), pltpu.VMEM((width, tokens), BF16),
                pltpu.VMEM((width, tile), F32),
            ],
        ),
        out_shape=(
            jax.ShapeDtypeStruct((tokens, width), F32),
            jax.ShapeDtypeStruct((half, up_rows, wider), BF16),
            jax.ShapeDtypeStruct((half, up_rows, wider), BF16),
            jax.ShapeDtypeStruct((8, width), F32),
        ),
        compiler_params=pltpu.CompilerParams(vmem_limit_bytes=VMEM_LIMIT),
        cost_estimate=pl.CostEstimate(
            flops=4 * tokens * width * wider, transcendentals=tokens, bytes_accessed=25 << 20
        ),
        name="feed_back",
    )(my_id(), second, back, upstream, middle, up, vectors)


def attend_back(x, across, down, weights, vectors, qkv, lse, dmid):
    tokens, width = x.shape
    slots = across.shape[2]
    rows = tokens // slots
    heads = width // HEAD_DIM

    def body(
        x_ref, across_ref, down_ref, w_ref, vec_ref, qkv_ref, lse_ref, dmid_ref,
        dx_ref, dqkv_ref, dattn_ref, sums,
        dctx,
    ):
        @pl.when(pl.program_id(0) == 0)
        def _():
            sums[...] = jnp.zeros_like(sums)

        middle_grad = dmid_ref[...]
        dattn = low(middle_grad)
        dattn_ref[...] = dattn
        dctx[...] = low(dot(dattn, w_ref[:, 3 * width : 4 * width], 1, 1))
        bias = mask_of(across_ref[0], down_ref[...])
        masks = halves()
        for pair in range(heads // 2):
            lanes = [slice(p * width + pair * PAIR, p * width + (pair + 1) * PAIR) for p in range(3)]
            q, k, v = (qkv_ref[:, lane] for lane in lanes)
            dout = dctx[:, lanes[0]]
            dq = jnp.zeros((slots, PAIR), F32)
            dk = jnp.zeros((slots, PAIR), F32)
            dv = jnp.zeros((slots, PAIR), F32)
            for side in range(2):
                head = 2 * pair + side
                q_half, dout_half = q * masks[side], dout * masks[side]
                scores = dot(q_half, k, 1, 1) * HEAD_DIM**-0.5 + bias
                probs = jnp.exp(scores - lse_ref[:, head : head + 1])
                dprobs = dot(dout_half, v, 1, 1)
                weighted = probs * dprobs
                dscores = low(weighted - probs * jnp.sum(weighted, axis=-1, keepdims=True))
                dv = dv + dot(low(probs), dout_half, 0, 0)
                dq = dq + dot(dscores, k * masks[side])
                dk = dk + dot(dscores, q_half, 0, 0)
            dqkv_ref[:, lanes[0]] = low(dq * HEAD_DIM**-0.5)
            dqkv_ref[:, lanes[1]] = low(dk * HEAD_DIM**-0.5)
            dqkv_ref[:, lanes[2]] = low(dv)
        dfirst = jnp.zeros((slots, width), F32)
        for p in range(3):
            part = slice(p * width, (p + 1) * width)
            dfirst = dfirst + dot(dqkv_ref[:, part], w_ref[:, part], 1, 1)
        unit, scale = normalized(wide(x_ref[...]))
        dx_ref[...] = low(middle_grad + norm_back(dfirst, unit, scale, vec_ref[0:1, :]))
        sums[0:1, :] += column_sums(dfirst * unit)
        sums[1:2, :] += column_sums(dfirst)
        sums[2:3, :] += column_sums(wide(dqkv_ref[:, :width]))
        sums[3:4, :] += column_sums(wide(dqkv_ref[:, 2 * width :]))
        sums[4:5, :] += column_sums(wide(dattn))

    def row(columns):
        return pl.BlockSpec((slots, columns), lambda i: (i, 0))

    def whole(array):
        return pl.BlockSpec(array.shape, lambda i: (0, 0), pipeline_mode=pl.Buffered(1))

    return pl.pallas_call(
        body,
        grid=(rows,),
        in_specs=[
            row(width),
            pl.BlockSpec((1, 1, slots), lambda i: (i, 0, 0)),
            row(1), whole(weights), whole(vectors), row(3 * width), row(heads), row(width),
        ],
        out_specs=(
            row(width), row(3 * width), row(width), pl.BlockSpec((8, width), lambda i: (0, 0))
        ),
        scratch_shapes=[pltpu.VMEM((slots, width), BF16)],
        out_shape=(
            jax.ShapeDtypeStruct((tokens, width), BF16),
            jax.ShapeDtypeStruct((tokens, 3 * width), BF16),
            jax.ShapeDtypeStruct((tokens, width), BF16),
            jax.ShapeDtypeStruct((8, width), F32),
        ),
        compiler_params=pltpu.CompilerParams(vmem_limit_bytes=VMEM_LIMIT),
        cost_estimate=pl.CostEstimate(
            flops=2 * tokens * width * width * 4 + 10 * rows * heads * slots * slots * HEAD_DIM,
            transcendentals=rows * heads * slots * slots,
            bytes_accessed=25 << 20,
        ),
        name="attend_back",
    )(x, across, down, weights, vectors, qkv, lse, dmid)


def attend_weights(first, dqkv, context, dattn, sums, mid_rows, down_rows, long_row, count):
    tokens, width = first.shape
    wider = long_row.shape[1]
    share, long_share = width // count, wider // count
    used = -(-(8 * share + long_share) // LANES)

    def body(
        id_ref, first_ref, dqkv_ref, ctx_ref, dattn_ref, sums_ref, mid_ref, last_ref, long_ref,
        keep_ref, send_ref, product,
    ):
        me = id_ref[0]
        turned = first_ref[...].T
        for p in range(4):
            part = slice(p * width, (p + 1) * width)
            if p < 3:
                product[...] = dot(turned, dqkv_ref[:, part])
            else:
                product[...] = dot(ctx_ref[...], dattn_ref[...], 0, 0)

            spread(
                product, share, count, me, keep_ref.at[:, :, part], send_ref.at[:, :, part]
            )

        def fold(row, shift, period):
            columns = row.shape[1]
            mine = low(jnp.where(owned(count, columns, period), row, 0.0))
            found = []
            for line in range(used):
                pick = same(LANES, columns, shift - line * LANES, period)
                found.append(dot(mine, low(pick.astype(F32)), 1, 1))
            return found

        lines = fold(long_ref[...], 8 * share, long_share)
        for v in range(8):
            source, line = ((sums_ref, v), (mid_ref, v - 5), (last_ref, 0))[(v > 4) + (v > 6)]
            row = source[line : line + 1, :]
            lines = [old + new for old, new in zip(lines, fold(row, v * share, share))]
        number = lax.broadcasted_iota(jnp.int32, (share, LANES), 0)

        def block_of(owner):
            block = jnp.zeros((share, LANES), F32)
            for line in range(used):
                block = jnp.where(number == line, lines[line][owner : owner + 1, :], block)
            return low(block)

        for couple in range(count // 2):
            slot = couple ^ (me // 2)
            even, odd = block_of(2 * couple), block_of(2 * couple + 1)
            keep_ref[slot, :, 4 * width :] = jnp.where(me % 2 == 0, even, odd)
            send_ref[slot, :, 4 * width :] = jnp.where(me % 2 == 0, odd, even)

    block = (count // 2, share, 4 * width + LANES)
    vmem = pl.BlockSpec(memory_space=pltpu.VMEM)
    return pl.pallas_call(
        body,
        in_specs=[pl.BlockSpec(memory_space=pltpu.SMEM)] + [vmem] * 8,
        out_specs=(vmem, vmem),
        out_shape=(jax.ShapeDtypeStruct(block, BF16), jax.ShapeDtypeStruct(block, BF16)),
        scratch_shapes=[pltpu.VMEM((width, width), F32)],
        compiler_params=pltpu.CompilerParams(vmem_limit_bytes=VMEM_LIMIT),
        cost_estimate=pl.CostEstimate(
            flops=2 * tokens * width * width * 4, transcendentals=0, bytes_accessed=15 << 20
        ),
        name="attend_weights",
    )(my_id(), first, dqkv, context, dattn, sums, mid_rows, down_rows, long_row)


def shards(
    layer_input, segments, cotangent, pre_gain, pre_shift, w_qkv, b_query, b_value, w_out, b_out,
    mid_gain, mid_shift, w_up, b_up, w_down, b_down,
):
    row_count, slot_count, width = layer_input.shape
    tokens = row_count * slot_count
    share, long_share = pre_gain.shape[0], b_up.shape[0]
    count = width // share
    small = [pre_gain, pre_shift, b_query, b_value, b_out, mid_gain, mid_shift, b_down, b_up]
    near = pack_near(w_qkv, w_out, small)

    near_pieces = gather_chips(near, count)
    up_pieces = gather_chips(low(w_up), count)
    down_pieces = gather_chips(low(w_down), count)
    near_all = gather_core(near_pieces, count)
    near_full = lay_out(near_all, count)

    x = layer_input.reshape(tokens, width)
    grads = cotangent.reshape(tokens, width)
    across = segments.reshape(row_count, 1, slot_count)
    down = segments.reshape(tokens, 1)
    vectors, long_bias = unpack_small(near_full, count, width, count * long_share)
    first, qkv, context, lse, middle, second = attend(x, across, down, near_full, vectors)
    up_full = lay_out(gather_core(up_pieces, count), count)
    down_full = lay_out(gather_core(down_pieces, count), count)
    result, back, down_keep, down_send, long_row, down_row = feed_forward(
        second, grads, middle, up_full, down_full, vectors, long_bias, count
    )
    dmid, up_keep, up_send, mid_rows = feed_back(
        second, back, grads, middle, up_full, vectors, count
    )
    down_total = reduce_blocks(down_keep, down_send, count)
    up_total = reduce_blocks(up_keep, up_send, count)
    dx, dqkv, dattn, sums = attend_back(x, across, down, near_full, vectors, qkv, lse, dmid)
    keep, send = attend_weights(
        first, dqkv, context, dattn, sums, mid_rows, down_row, long_row, count
    )
    total = reduce_blocks(keep, send, count)
    used = -(-(8 * share + long_share) // LANES)
    flat = total[:used, 4 * width :].reshape(-1)
    vector_grads = [flat[v * share : (v + 1) * share] for v in range(8)]
    return (
        result.reshape(layer_input.shape),
        dx.reshape(layer_input.shape),
        vector_grads[0],
        vector_grads[1],
        total[:, : 3 * width],
        vector_grads[2],
        vector_grads[3],
        total[:, 3 * width : 4 * width],
        vector_grads[4],
        vector_grads[5],
        vector_grads[6],
        up_total,
        flat[8 * share : 8 * share + long_share],
        down_total,
        vector_grads[7],
    )


def solution(mesh):
    line, table = P(AXIS), P(AXIS, None)
    cube = P(AXIS, None, None)
    return jax.shard_map(
        shards,
        mesh=mesh,
        in_specs=(
            cube, table, cube, line, line, table, line, line, table, line, line, line, table, line,
            table, line,
        ),
        out_specs=(
            cube, cube, line, line, table, line, line, table, line, line, line, table, line, table,
            line,
        ),
        check_vma=False,
    )
```

```python
import jax
import jax.numpy as jnp
from jax import lax
from jax.experimental import pallas as pl
from jax.experimental.pallas import tpu as pltpu
from jax.sharding import PartitionSpec as P

HEAD_DIM = 64
PAIR = 2 * HEAD_DIM
LANES = 128
EPSILON = 1e-06
BLOCKED = -1e9
AXIS = "fsdp"
FF_TILE = 384
GROUP = 2
VMEM_LIMIT = 60 << 20
F32 = jnp.float32
BF16 = jnp.bfloat16


def wide(value):
    return value.astype(F32)


def low(value):
    return value.astype(BF16)


def dot(left, right, left_dim=1, right_dim=0):
    return lax.dot_general(
        left, right, (((left_dim,), (right_dim,)), ((), ())), preferred_element_type=F32
    )


def axes_of(count):
    rest = count.bit_length() - 2
    side = rest // 3
    return (1 << side, 1), (1 << side, 1 + side), (1 << (rest - 2 * side), 1 + 2 * side)


def swap(value, mask, count):
    return lax.ppermute(value, AXIS, [(i, i ^ mask) for i in range(count)])


def my_id():
    return lax.axis_index(AXIS).astype(jnp.int32)[None]


def gather(value, axis, count):
    size, bit = axis
    return [value] + [swap(value, d << bit, count) for d in range(1, size)]


def gather_chips(shard, count):
    x, y, z = axes_of(count)
    column = jnp.stack(gather(shard, z, count))
    half = z[0] // 2
    left = jnp.stack(gather(column[:half], x, count))
    right = jnp.stack(gather(column[half:], y, count))
    return gather(left, y, count) + gather(right, x, count)


def gather_core(pieces, count):
    return pieces + [swap(piece, 1, count) for piece in pieces]


def lay_out(pieces, count):
    (xs, xbit), (ys, ybit), (zs, zbit) = axes_of(count)
    block = pieces[0].shape[2:]
    half = zs // 2

    def body(id_ref, *refs):
        sources, out, sems = refs[: len(pieces)], refs[-2], refs[-1]
        copies = []
        for index, source in enumerate(sources):
            c, place = divmod(index, ys + xs)
            for inner in range(source.shape[0]):
                for m in range(half):
                    if place < ys:
                        block_id = c | inner << xbit | place << ybit | m << zbit
                    else:
                        block_id = c | (place - ys) << xbit | inner << ybit | (m + half) << zbit
                    copy = pltpu.make_async_copy(
                        source.at[inner, m], out.at[id_ref[0] ^ block_id], sems.at[len(copies)]
                    )
                    copy.start()
                    copies.append(copy)
        for copy in copies:
            copy.wait()

    full = pl.pallas_call(
        body,
        out_shape=jax.ShapeDtypeStruct((count,) + block, pieces[0].dtype),
        in_specs=[pl.BlockSpec(memory_space=pltpu.SMEM)]
        + [pl.BlockSpec(memory_space=pl.ANY)] * len(pieces),
        out_specs=pl.BlockSpec(memory_space=pltpu.VMEM),
        scratch_shapes=[pltpu.SemaphoreType.DMA((count,))],
        name="lay_out",
    )(my_id(), *pieces)
    return full.reshape((count * block[0],) + block[1:])


def reduce_axis(parts, axis, count):
    size, bit = axis
    total = wide(parts[0])
    for d in range(1, size):
        total = total + wide(swap(parts[d], d << bit, count))
    return total


def reduce_blocks(keep, send, count):
    x, y, z = axes_of(count)
    shape = (z[0], y[0], x[0]) + keep.shape[1:]
    both = wide(keep) + wide(swap(send, 1, count))
    both = low(both).reshape(shape)
    half = z[0] // 2
    left = [both[:half, :, d] for d in range(x[0])]
    left = low(reduce_axis(left, x, count))
    right = [both[half:, d] for d in range(y[0])]
    right = low(reduce_axis(right, y, count))
    left = low(reduce_axis([left[:, d] for d in range(y[0])], y, count))
    right = low(reduce_axis([right[:, d] for d in range(x[0])], x, count))
    column = [left[m] for m in range(half)] + [right[m] for m in range(half)]
    return reduce_axis(column, z, count)


def same(rows, columns, shift, period):
    row = lax.broadcasted_iota(jnp.int32, (rows, columns), 0)
    column = lax.broadcasted_iota(jnp.int32, (rows, columns), 1)
    return row == shift + column % period


def owned(count, columns, share):
    row = lax.broadcasted_iota(jnp.int32, (count, columns), 0)
    column = lax.broadcasted_iota(jnp.int32, (count, columns), 1)
    return row == column // share


def pack_near(qkv, out, vectors):
    rows = qkv.shape[0]
    sizes = [vector.shape[0] for vector in vectors]
    used = -(-sum(sizes) // LANES)
    columns = qkv.shape[1] + out.shape[1] + LANES

    def body(qkv_ref, out_ref, *refs):
        near_ref = refs[-1]
        near_ref[:, : qkv.shape[1]] = low(qkv_ref[...])
        near_ref[:, qkv.shape[1] : columns - LANES] = low(out_ref[...])
        number = lax.broadcasted_iota(jnp.int32, (rows, LANES), 0)
        block = jnp.zeros((rows, LANES), F32)
        for line in range(used):
            text, start = jnp.zeros((8, LANES), F32), 0
            for ref, size in zip(refs, sizes):
                if start < (line + 1) * LANES and start + size > line * LANES:
                    column = lax.broadcasted_iota(jnp.int32, (size, LANES), 1)
                    row = lax.broadcasted_iota(jnp.int32, (size, LANES), 0)
                    pick = low((column == row + (start - line * LANES)).astype(F32))
                    text = text + dot(low(jnp.broadcast_to(ref[...], (8, size))), pick)
                start += size
            block = jnp.where(number == line, text[:1], block)
        near_ref[:, columns - LANES :] = low(block)

    vmem = pl.BlockSpec(memory_space=pltpu.VMEM)
    return pl.pallas_call(
        body,
        out_shape=jax.ShapeDtypeStruct((rows, columns), BF16),
        in_specs=[vmem] * (2 + len(vectors)),
        out_specs=vmem,
        name="pack_near",
    )(qkv, out, *[vector.reshape(1, -1) for vector in vectors])


def unpack_small(weights, count, width, wider):
    rows = width // count
    share, long_share = rows, wider // count
    used = -(-(8 * share + long_share) // LANES)

    def body(block_ref, vectors_ref, long_ref):
        block = wide(block_ref[...]).reshape(count, rows, LANES)
        flat = [low(block[:, line, :]) for line in range(used)]

        def spread(shift, period, columns):
            total = jnp.zeros((count, columns), F32)
            for line in range(used):
                pick = same(LANES, columns, shift - line * LANES, period)
                total = total + dot(flat[line], low(pick.astype(F32)))
            mine = jnp.where(owned(count, columns, period), total, 0.0)
            return jnp.sum(mine, axis=0, keepdims=True)

        for v in range(8):
            vectors_ref[v : v + 1, :] = spread(v * share, share, width)
        long_ref[...] = spread(8 * share, long_share, wider)

    return pl.pallas_call(
        body,
        grid=(1,),
        out_shape=(jax.ShapeDtypeStruct((8, width), F32), jax.ShapeDtypeStruct((1, wider), F32)),
        in_specs=[pl.BlockSpec((width, LANES), lambda i: (0, weights.shape[1] // LANES - 1))],
        out_specs=(
            pl.BlockSpec((8, width), lambda i: (0, 0)),
            pl.BlockSpec((1, wider), lambda i: (0, 0)),
        ),
        name="unpack_small",
    )(weights)


def normalized(value):
    centred = value - jnp.mean(value, axis=-1, keepdims=True)
    scale = lax.rsqrt(jnp.mean(centred * centred, axis=-1, keepdims=True) + EPSILON)
    return centred * scale, scale


def norm_back(grad, unit, scale, gain):
    inner = grad * gain
    average = jnp.mean(inner, axis=-1, keepdims=True)
    along = jnp.mean(inner * unit, axis=-1, keepdims=True)
    return scale * (inner - average - unit * along)


def column_sums(value):
    return jnp.sum(value, axis=0, keepdims=True)


def halves():
    lane = lax.broadcasted_iota(jnp.int32, (1, PAIR), 1)
    first = low((lane < HEAD_DIM).astype(F32))
    return first, low((lane >= HEAD_DIM).astype(F32))


def mask_of(across, down):
    slots = across.shape[1]
    row = lax.broadcasted_iota(jnp.int32, (slots, slots), 0)
    column = lax.broadcasted_iota(jnp.int32, (slots, slots), 1)
    allowed = ((down == across) & (down > 0)) | (row == column)
    return jnp.where(allowed, 0.0, BLOCKED)


def spread(product, rows, count, me, keep, send):
    if rows % 8 == 0:

        def place(slot, carry):
            for c, out in enumerate((keep, send)):
                start = pl.multiple_of((me ^ (2 * slot + c)) * rows, 8)
                out[slot] = low(product[pl.ds(start, rows), :])
            return carry

        lax.fori_loop(0, count // 2, place, 0)
        return
    for couple in range(count // 2):
        slot = couple ^ (me // 2)
        even = low(product[2 * couple * rows : (2 * couple + 1) * rows, :])
        odd = low(product[(2 * couple + 1) * rows : (2 * couple + 2) * rows, :])
        keep[slot] = jnp.where(me % 2 == 0, even, odd)
        send[slot] = jnp.where(me % 2 == 0, odd, even)


def attend(x, across, down, weights, vectors):
    tokens, width = x.shape
    slots = across.shape[2]
    rows = tokens // slots
    heads = width // HEAD_DIM

    def body(x_ref, across_ref, down_ref, w_ref, vec_ref, first_ref, qkv_ref, ctx_ref, lse_ref, mid_ref, second_ref):
        value = wide(x_ref[...])
        unit, _ = normalized(value)
        first = low(unit * vec_ref[0:1, :] + vec_ref[1:2, :])
        first_ref[...] = first
        for part in range(3):
            product = dot(first, w_ref[:, part * width : (part + 1) * width])
            if part != 1:
                product = product + vec_ref[2 + part // 2 : 3 + part // 2, :]
            qkv_ref[:, part * width : (part + 1) * width] = low(product)
        bias = mask_of(across_ref[0], down_ref[...])
        masks = halves()
        place = lax.broadcasted_iota(jnp.int32, (slots, heads), 1)

        def couple(pair, found):
            def lanes(part):
                return pl.ds(pl.multiple_of(part * width + pair * PAIR, PAIR), PAIR)

            q, k, v = (qkv_ref[:, lanes(part)] for part in range(3))
            context = jnp.zeros((slots, PAIR), F32)
            for side in range(2):
                scores = dot(q * masks[side], k, 1, 1) * HEAD_DIM**-0.5 + bias
                highest = jnp.max(scores, axis=-1, keepdims=True)
                powers = jnp.exp(scores - highest)
                total = jnp.sum(powers, axis=-1, keepdims=True)
                probs = low(powers * (1.0 / total))
                context = context + dot(probs, v * masks[side])
                found = jnp.where(place == 2 * pair + side, highest + jnp.log(total), found)
            ctx_ref[:, lanes(0)] = low(context)
            return found

        def several(step, found):
            for offset in range(GROUP):
                found = couple(step * GROUP + offset, found)
            return found

        lse_ref[...] = lax.fori_loop(
            0, heads // 2 // GROUP, several, jnp.zeros((slots, heads), F32)
        )
        attention = dot(ctx_ref[...], w_ref[:, 3 * width : 4 * width]) + vec_ref[4:5, :]
        middle = value + attention
        mid_ref[...] = middle
        unit, _ = normalized(middle)
        second_ref[...] = low(unit * vec_ref[5:6, :] + vec_ref[6:7, :])

    def row(columns):
        return pl.BlockSpec((slots, columns), lambda i: (i, 0))

    def whole(array):
        return pl.BlockSpec(array.shape, lambda i: (0, 0), pipeline_mode=pl.Buffered(1))

    shapes = [(width, BF16), (3 * width, BF16), (width, BF16), (heads, F32), (width, F32), (width, BF16)]
    return pl.pallas_call(
        body,
        grid=(rows,),
        out_shape=tuple(jax.ShapeDtypeStruct((tokens, c), t) for c, t in shapes),
        in_specs=[
            row(width),
            pl.BlockSpec((1, 1, slots), lambda i: (i, 0, 0)),
            row(1),
            whole(weights),
            whole(vectors),
        ],
        out_specs=tuple(row(c) for c, _ in shapes),
        compiler_params=pltpu.CompilerParams(vmem_limit_bytes=VMEM_LIMIT),
        cost_estimate=pl.CostEstimate(
            flops=2 * tokens * width * width * 4 + 4 * rows * heads * slots * slots * HEAD_DIM,
            transcendentals=rows * heads * slots * slots,
            bytes_accessed=30 << 20,
        ),
        name="attend",
    )(x, across, down, weights, vectors)


def feed_forward(second, upstream, middle, up, down, vectors, long_bias, count):
    tokens, width = second.shape
    wider = up.shape[1]
    tile = FF_TILE
    steps = wider // tile
    down_rows = wider // count
    group = tile // down_rows

    def body(
        id_ref, second_ref, grad_ref, mid_ref, up_ref, down_ref, vec_ref, bias_ref,
        out_ref, back_ref, down_keep, down_send, long_ref, rows_ref,
        out_sum, down_product,
    ):
        step = pl.program_id(0)
        me = id_ref[0]

        @pl.when(step == 0)
        def _():
            out_sum[...] = jnp.zeros_like(out_sum)

        grads = grad_ref[...]
        hidden = dot(second_ref[...], up_ref[...]) + bias_ref[...]
        below = 0.5 * (1.0 + lax.erf(hidden * 0.7071067811865476))
        active = low(hidden * below)
        slope = below + hidden * (jnp.exp(hidden * hidden * -0.5) * 0.3989422804014327)
        back = low(dot(grads, down_ref[...], 1, 1) * slope)
        back_ref[...] = back
        long_ref[...] = column_sums(wide(back))
        out_sum[...] += dot(active, down_ref[...])
        down_product[...] = dot(active, grads, 0, 0)
        spread(down_product, down_rows, group, me % group, down_keep, down_send)

        @pl.when(step == steps - 1)
        def _():
            out_ref[...] = low(mid_ref[...] + (out_sum[...] + vec_ref[7:8, :]))
            rows_ref[...] = jnp.broadcast_to(column_sums(wide(grads)), (8, width))

    def whole(array):
        return pl.BlockSpec(array.shape, lambda i, m: (0, 0), pipeline_mode=pl.Buffered(1))

    half = count // 2
    down_spec = pl.BlockSpec((group // 2, down_rows, width), lambda i, m: (i ^ (m[0] // group), 0, 0))
    return pl.pallas_call(
        body,
        grid_spec=pltpu.PrefetchScalarGridSpec(
            num_scalar_prefetch=1,
            grid=(steps,),
            in_specs=[
                whole(second), whole(upstream), whole(middle),
                pl.BlockSpec((width, tile), lambda i, m: (0, i)),
                pl.BlockSpec((tile, width), lambda i, m: (i, 0)),
                whole(vectors),
                pl.BlockSpec((1, tile), lambda i, m: (0, i)),
            ],
            out_specs=(
                pl.BlockSpec((tokens, width), lambda i, m: (0, 0)),
                pl.BlockSpec((tokens, tile), lambda i, m: (0, i)),
                down_spec, down_spec,
                pl.BlockSpec((1, tile), lambda i, m: (0, i)),
                pl.BlockSpec((8, width), lambda i, m: (0, 0)),
            ),
            scratch_shapes=[pltpu.VMEM((tokens, width), F32), pltpu.VMEM((tile, width), F32)],
        ),
        out_shape=(
            jax.ShapeDtypeStruct((tokens, width), BF16),
            jax.ShapeDtypeStruct((tokens, wider), BF16),
            jax.ShapeDtypeStruct((half, down_rows, width), BF16),
            jax.ShapeDtypeStruct((half, down_rows, width), BF16),
            jax.ShapeDtypeStruct((1, wider), F32),
            jax.ShapeDtypeStruct((8, width), F32),
        ),
        compiler_params=pltpu.CompilerParams(vmem_limit_bytes=VMEM_LIMIT),
        cost_estimate=pl.CostEstimate(
            flops=8 * tokens * width * wider, transcendentals=2 * tokens * wider,
            bytes_accessed=30 << 20,
        ),
        name="feed_forward",
    )(my_id(), second, upstream, middle, up, down, vectors, long_bias)


def feed_back(second, back, upstream, middle, up, vectors, count):
    tokens, width = second.shape
    wider = up.shape[1]
    tile = FF_TILE
    steps = wider // tile
    up_rows = width // count

    def body(
        id_ref, second_ref, back_ref, grad_ref, mid_ref, up_ref, vec_ref,
        dmid_ref, up_keep, up_send, rows_ref,
        back_sum, second_turned, up_product,
    ):
        step = pl.program_id(0)

        @pl.when(step == 0)
        def _():
            second_turned[...] = second_ref[...].T
            back_sum[...] = jnp.zeros_like(back_sum)

        back_sum[...] += dot(back_ref[...], up_ref[...], 1, 1)
        up_product[...] = dot(second_turned[...], back_ref[...])
        spread(up_product, up_rows, count, id_ref[0], up_keep, up_send)

        @pl.when(step == steps - 1)
        def _():
            unit, scale = normalized(mid_ref[...])
            da = back_sum[...]
            dmid_ref[...] = wide(grad_ref[...]) + norm_back(da, unit, scale, vec_ref[5:6, :])
            rows_ref[...] = jnp.zeros_like(rows_ref)
            rows_ref[0:1, :] = column_sums(da * unit)
            rows_ref[1:2, :] = column_sums(da)

    def whole(array):
        return pl.BlockSpec(array.shape, lambda i, m: (0, 0), pipeline_mode=pl.Buffered(1))

    half = count // 2
    up_spec = pl.BlockSpec((half, up_rows, tile), lambda i, m: (0, 0, i))
    return pl.pallas_call(
        body,
        grid_spec=pltpu.PrefetchScalarGridSpec(
            num_scalar_prefetch=1,
            grid=(steps,),
            in_specs=[
                whole(second),
                pl.BlockSpec((tokens, tile), lambda i, m: (0, i)),
                whole(upstream), whole(middle),
                pl.BlockSpec((width, tile), lambda i, m: (0, i)),
                whole(vectors),
            ],
            out_specs=(
                pl.BlockSpec((tokens, width), lambda i, m: (0, 0)),
                up_spec, up_spec,
                pl.BlockSpec((8, width), lambda i, m: (0, 0)),
            ),
            scratch_shapes=[
                pltpu.VMEM((tokens, width), F32), pltpu.VMEM((width, tokens), BF16),
                pltpu.VMEM((width, tile), F32),
            ],
        ),
        out_shape=(
            jax.ShapeDtypeStruct((tokens, width), F32),
            jax.ShapeDtypeStruct((half, up_rows, wider), BF16),
            jax.ShapeDtypeStruct((half, up_rows, wider), BF16),
            jax.ShapeDtypeStruct((8, width), F32),
        ),
        compiler_params=pltpu.CompilerParams(vmem_limit_bytes=VMEM_LIMIT),
        cost_estimate=pl.CostEstimate(
            flops=4 * tokens * width * wider, transcendentals=tokens, bytes_accessed=25 << 20
        ),
        name="feed_back",
    )(my_id(), second, back, upstream, middle, up, vectors)


def attend_back(x, across, down, weights, vectors, qkv, lse, dmid):
    tokens, width = x.shape
    slots = across.shape[2]
    rows = tokens // slots
    heads = width // HEAD_DIM

    def body(
        x_ref, across_ref, down_ref, w_ref, vec_ref, qkv_ref, lse_ref, dmid_ref,
        dx_ref, dqkv_ref, dattn_ref, sums,
        dctx,
    ):
        @pl.when(pl.program_id(0) == 0)
        def _():
            sums[...] = jnp.zeros_like(sums)

        middle_grad = dmid_ref[...]
        dattn = low(middle_grad)
        dattn_ref[...] = dattn
        dctx[...] = low(dot(dattn, w_ref[:, 3 * width : 4 * width], 1, 1))
        bias = mask_of(across_ref[0], down_ref[...])
        masks = halves()
        place = lax.broadcasted_iota(jnp.int32, (slots, heads), 1)

        def couple(pair):
            def lanes(part):
                return pl.ds(pl.multiple_of(part * width + pair * PAIR, PAIR), PAIR)

            mine = pl.ds(0, slots)
            q, k, v = (qkv_ref[mine, lanes(part)] for part in range(3))
            dout = dctx[:, lanes(0)]
            dq = jnp.zeros((slots, PAIR), F32)
            dk = jnp.zeros((slots, PAIR), F32)
            dv = jnp.zeros((slots, PAIR), F32)
            for side in range(2):
                kept = jnp.where(place == 2 * pair + side, lse_ref[...], 0.0)
                kept = jnp.sum(kept, axis=-1, keepdims=True)
                q_half, dout_half = q * masks[side], dout * masks[side]
                scores = dot(q_half, k, 1, 1) * HEAD_DIM**-0.5 + bias
                probs = jnp.exp(scores - kept)
                dprobs = dot(dout_half, v, 1, 1)
                weighted = probs * dprobs
                dscores = low(weighted - probs * jnp.sum(weighted, axis=-1, keepdims=True))
                dv = dv + dot(low(probs), dout_half, 0, 0)
                dq = dq + dot(dscores, k * masks[side])
                dk = dk + dot(dscores, q_half, 0, 0)
            dqkv_ref[:, lanes(0)] = low(dq * HEAD_DIM**-0.5)
            dqkv_ref[:, lanes(1)] = low(dk * HEAD_DIM**-0.5)
            dqkv_ref[:, lanes(2)] = low(dv)

        def several(step, carry):
            for offset in range(GROUP):
                couple(step * GROUP + offset)
            return carry

        lax.fori_loop(0, heads // 2 // GROUP, several, 0)
        dfirst = jnp.zeros((slots, width), F32)
        for p in range(3):
            part = slice(p * width, (p + 1) * width)
            dfirst = dfirst + dot(dqkv_ref[:, part], w_ref[:, part], 1, 1)
        unit, scale = normalized(wide(x_ref[...]))
        dx_ref[...] = low(middle_grad + norm_back(dfirst, unit, scale, vec_ref[0:1, :]))
        sums[0:1, :] += column_sums(dfirst * unit)
        sums[1:2, :] += column_sums(dfirst)
        sums[2:3, :] += column_sums(wide(dqkv_ref[:, :width]))
        sums[3:4, :] += column_sums(wide(dqkv_ref[:, 2 * width :]))
        sums[4:5, :] += column_sums(wide(dattn))

    def row(columns):
        return pl.BlockSpec((slots, columns), lambda i: (i, 0))

    def whole(array):
        return pl.BlockSpec(array.shape, lambda i: (0, 0), pipeline_mode=pl.Buffered(1))

    return pl.pallas_call(
        body,
        grid=(rows,),
        in_specs=[
            row(width),
            pl.BlockSpec((1, 1, slots), lambda i: (i, 0, 0)),
            row(1), whole(weights), whole(vectors), row(3 * width), row(heads), row(width),
        ],
        out_specs=(
            row(width), row(3 * width), row(width), pl.BlockSpec((8, width), lambda i: (0, 0))
        ),
        scratch_shapes=[pltpu.VMEM((slots, width), BF16)],
        out_shape=(
            jax.ShapeDtypeStruct((tokens, width), BF16),
            jax.ShapeDtypeStruct((tokens, 3 * width), BF16),
            jax.ShapeDtypeStruct((tokens, width), BF16),
            jax.ShapeDtypeStruct((8, width), F32),
        ),
        compiler_params=pltpu.CompilerParams(vmem_limit_bytes=VMEM_LIMIT),
        cost_estimate=pl.CostEstimate(
            flops=2 * tokens * width * width * 4 + 10 * rows * heads * slots * slots * HEAD_DIM,
            transcendentals=rows * heads * slots * slots,
            bytes_accessed=25 << 20,
        ),
        name="attend_back",
    )(x, across, down, weights, vectors, qkv, lse, dmid)


def attend_weights(first, dqkv, context, dattn, sums, mid_rows, down_rows, long_row, count):
    tokens, width = first.shape
    wider = long_row.shape[1]
    share, long_share = width // count, wider // count
    used = -(-(8 * share + long_share) // LANES)

    def body(
        id_ref, first_ref, dqkv_ref, ctx_ref, dattn_ref, sums_ref, mid_ref, last_ref, long_ref,
        keep_ref, send_ref, product,
    ):
        me = id_ref[0]
        turned = first_ref[...].T
        for p in range(4):
            part = slice(p * width, (p + 1) * width)
            if p < 3:
                product[...] = dot(turned, dqkv_ref[:, part])
            else:
                product[...] = dot(ctx_ref[...], dattn_ref[...], 0, 0)

            spread(
                product, share, count, me, keep_ref.at[:, :, part], send_ref.at[:, :, part]
            )

        def fold(row, shift, period):
            columns = row.shape[1]
            mine = low(jnp.where(owned(count, columns, period), row, 0.0))
            found = []
            for line in range(used):
                pick = same(LANES, columns, shift - line * LANES, period)
                found.append(dot(mine, low(pick.astype(F32)), 1, 1))
            return found

        lines = fold(long_ref[...], 8 * share, long_share)
        for v in range(8):
            source, line = ((sums_ref, v), (mid_ref, v - 5), (last_ref, 0))[(v > 4) + (v > 6)]
            row = source[line : line + 1, :]
            lines = [old + new for old, new in zip(lines, fold(row, v * share, share))]
        number = lax.broadcasted_iota(jnp.int32, (share, LANES), 0)

        def block_of(owner):
            block = jnp.zeros((share, LANES), F32)
            for line in range(used):
                block = jnp.where(number == line, lines[line][owner : owner + 1, :], block)
            return low(block)

        for couple in range(count // 2):
            slot = couple ^ (me // 2)
            even, odd = block_of(2 * couple), block_of(2 * couple + 1)
            keep_ref[slot, :, 4 * width :] = jnp.where(me % 2 == 0, even, odd)
            send_ref[slot, :, 4 * width :] = jnp.where(me % 2 == 0, odd, even)

    block = (count // 2, share, 4 * width + LANES)
    vmem = pl.BlockSpec(memory_space=pltpu.VMEM)
    return pl.pallas_call(
        body,
        in_specs=[pl.BlockSpec(memory_space=pltpu.SMEM)] + [vmem] * 8,
        out_specs=(vmem, vmem),
        out_shape=(jax.ShapeDtypeStruct(block, BF16), jax.ShapeDtypeStruct(block, BF16)),
        scratch_shapes=[pltpu.VMEM((width, width), F32)],
        compiler_params=pltpu.CompilerParams(vmem_limit_bytes=VMEM_LIMIT),
        cost_estimate=pl.CostEstimate(
            flops=2 * tokens * width * width * 4, transcendentals=0, bytes_accessed=15 << 20
        ),
        name="attend_weights",
    )(my_id(), first, dqkv, context, dattn, sums, mid_rows, down_rows, long_row)


def shards(
    layer_input, segments, cotangent, pre_gain, pre_shift, w_qkv, b_query, b_value, w_out, b_out,
    mid_gain, mid_shift, w_up, b_up, w_down, b_down,
):
    row_count, slot_count, width = layer_input.shape
    tokens = row_count * slot_count
    share, long_share = pre_gain.shape[0], b_up.shape[0]
    count = width // share
    small = [pre_gain, pre_shift, b_query, b_value, b_out, mid_gain, mid_shift, b_down, b_up]
    near = pack_near(w_qkv, w_out, small)

    near_pieces = gather_chips(near, count)
    up_pieces = gather_chips(low(w_up), count)
    down_pieces = gather_chips(low(w_down), count)
    near_all = gather_core(near_pieces, count)
    near_full = lay_out(near_all, count)

    x = layer_input.reshape(tokens, width)
    grads = cotangent.reshape(tokens, width)
    across = segments.reshape(row_count, 1, slot_count)
    down = segments.reshape(tokens, 1)
    vectors, long_bias = unpack_small(near_full, count, width, count * long_share)
    first, qkv, context, lse, middle, second = attend(x, across, down, near_full, vectors)
    up_full = lay_out(gather_core(up_pieces, count), count)
    down_full = lay_out(gather_core(down_pieces, count), count)
    result, back, down_keep, down_send, long_row, down_row = feed_forward(
        second, grads, middle, up_full, down_full, vectors, long_bias, count
    )
    dmid, up_keep, up_send, mid_rows = feed_back(
        second, back, grads, middle, up_full, vectors, count
    )
    down_total = reduce_blocks(down_keep, down_send, count)
    up_total = reduce_blocks(up_keep, up_send, count)
    dx, dqkv, dattn, sums = attend_back(x, across, down, near_full, vectors, qkv, lse, dmid)
    keep, send = attend_weights(
        first, dqkv, context, dattn, sums, mid_rows, down_row, long_row, count
    )
    total = reduce_blocks(keep, send, count)
    used = -(-(8 * share + long_share) // LANES)
    flat = total[:used, 4 * width :].reshape(-1)
    vector_grads = [flat[v * share : (v + 1) * share] for v in range(8)]
    return (
        result.reshape(layer_input.shape),
        dx.reshape(layer_input.shape),
        vector_grads[0],
        vector_grads[1],
        total[:, : 3 * width],
        vector_grads[2],
        vector_grads[3],
        total[:, 3 * width : 4 * width],
        vector_grads[4],
        vector_grads[5],
        vector_grads[6],
        up_total,
        flat[8 * share : 8 * share + long_share],
        down_total,
        vector_grads[7],
    )


def solution(mesh):
    line, table = P(AXIS), P(AXIS, None)
    cube = P(AXIS, None, None)
    return jax.shard_map(
        shards,
        mesh=mesh,
        in_specs=(
            cube, table, cube, line, line, table, line, line, table, line, line, line, table, line,
            table, line,
        ),
        out_specs=(
            cube, cube, line, line, table, line, line, table, line, line, line, table, line, table,
            line,
        ),
        check_vma=False,
    )
```

```python
import jax
import jax.numpy as jnp
from jax import lax
from jax.experimental import pallas as pl
from jax.experimental.pallas import tpu as pltpu
from jax.sharding import PartitionSpec as P

HEAD_DIM = 64
PAIR = 2 * HEAD_DIM
LANES = 128
EPSILON = 1e-06
BLOCKED = -1e9
AXIS = "fsdp"
FF_TILE = 768
GROUP = 2
VMEM_LIMIT = 60 << 20
F32 = jnp.float32
BF16 = jnp.bfloat16


def wide(value):
    return value.astype(F32)


def low(value):
    return value.astype(BF16)


def dot(left, right, left_dim=1, right_dim=0):
    return lax.dot_general(
        left, right, (((left_dim,), (right_dim,)), ((), ())), preferred_element_type=F32
    )


def axes_of(count):
    rest = count.bit_length() - 2
    side = rest // 3
    return (1 << side, 1), (1 << side, 1 + side), (1 << (rest - 2 * side), 1 + 2 * side)


def swap(value, mask, count):
    return lax.ppermute(value, AXIS, [(i, i ^ mask) for i in range(count)])


def my_id():
    return lax.axis_index(AXIS).astype(jnp.int32)[None]


def gather(value, axis, count):
    size, bit = axis
    return [value] + [swap(value, d << bit, count) for d in range(1, size)]


def gather_chips(shard, count):
    x, y, z = axes_of(count)
    column = jnp.stack(gather(shard, z, count))
    half = z[0] // 2
    left = jnp.stack(gather(column[:half], x, count))
    right = jnp.stack(gather(column[half:], y, count))
    return gather(left, y, count) + gather(right, x, count)


def gather_core(pieces, count):
    return pieces + [swap(piece, 1, count) for piece in pieces]


def lay_out(pieces, count):
    (xs, xbit), (ys, ybit), (zs, zbit) = axes_of(count)
    block = pieces[0].shape[2:]
    half = zs // 2

    def body(id_ref, *refs):
        sources, out, sems = refs[: len(pieces)], refs[-2], refs[-1]
        copies = []
        for index, source in enumerate(sources):
            c, place = divmod(index, ys + xs)
            for inner in range(source.shape[0]):
                for m in range(half):
                    if place < ys:
                        block_id = c | inner << xbit | place << ybit | m << zbit
                    else:
                        block_id = c | (place - ys) << xbit | inner << ybit | (m + half) << zbit
                    copy = pltpu.make_async_copy(
                        source.at[inner, m], out.at[id_ref[0] ^ block_id], sems.at[len(copies)]
                    )
                    copy.start()
                    copies.append(copy)
        for copy in copies:
            copy.wait()

    full = pl.pallas_call(
        body,
        out_shape=jax.ShapeDtypeStruct((count,) + block, pieces[0].dtype),
        in_specs=[pl.BlockSpec(memory_space=pltpu.SMEM)]
        + [pl.BlockSpec(memory_space=pl.ANY)] * len(pieces),
        out_specs=pl.BlockSpec(memory_space=pltpu.VMEM),
        scratch_shapes=[pltpu.SemaphoreType.DMA((count,))],
        name="lay_out",
    )(my_id(), *pieces)
    return full.reshape((count * block[0],) + block[1:])


def reduce_axis(parts, axis, count):
    size, bit = axis
    total = wide(parts[0])
    for d in range(1, size):
        total = total + wide(swap(parts[d], d << bit, count))
    return total


def reduce_blocks(keep, send, count):
    x, y, z = axes_of(count)
    shape = (z[0], y[0], x[0]) + keep.shape[1:]
    other = swap(send, 1, count)
    both = low(wide(keep) + wide(other)).reshape(shape)
    half = z[0] // 2
    left = [both[:half, :, d] for d in range(x[0])]
    left = low(reduce_axis(left, x, count))
    right = [both[half:, d] for d in range(y[0])]
    right = low(reduce_axis(right, y, count))
    left = low(reduce_axis([left[:, d] for d in range(y[0])], y, count))
    right = low(reduce_axis([right[:, d] for d in range(x[0])], x, count))
    column = [left[m] for m in range(half)] + [right[m] for m in range(half)]
    return reduce_axis(column, z, count)


def same(rows, columns, shift, period):
    row = lax.broadcasted_iota(jnp.int32, (rows, columns), 0)
    column = lax.broadcasted_iota(jnp.int32, (rows, columns), 1)
    return row == shift + column % period


def owned(count, columns, share):
    row = lax.broadcasted_iota(jnp.int32, (count, columns), 0)
    column = lax.broadcasted_iota(jnp.int32, (count, columns), 1)
    return row == column // share


def pack_near(qkv, out, vectors):
    rows = qkv.shape[0]
    sizes = [vector.shape[0] for vector in vectors]
    used = -(-sum(sizes) // LANES)
    columns = qkv.shape[1] + out.shape[1] + LANES

    def body(qkv_ref, out_ref, *refs):
        near_ref = refs[-1]
        near_ref[:, : qkv.shape[1]] = low(qkv_ref[...])
        near_ref[:, qkv.shape[1] : columns - LANES] = low(out_ref[...])
        number = lax.broadcasted_iota(jnp.int32, (rows, LANES), 0)
        block = jnp.zeros((rows, LANES), F32)
        for line in range(used):
            text, start = jnp.zeros((8, LANES), F32), 0
            for ref, size in zip(refs, sizes):
                if start < (line + 1) * LANES and start + size > line * LANES:
                    column = lax.broadcasted_iota(jnp.int32, (size, LANES), 1)
                    row = lax.broadcasted_iota(jnp.int32, (size, LANES), 0)
                    pick = low((column == row + (start - line * LANES)).astype(F32))
                    text = text + dot(low(jnp.broadcast_to(ref[...], (8, size))), pick)
                start += size
            block = jnp.where(number == line, text[:1], block)
        near_ref[:, columns - LANES :] = low(block)

    vmem = pl.BlockSpec(memory_space=pltpu.VMEM)
    return pl.pallas_call(
        body,
        out_shape=jax.ShapeDtypeStruct((rows, columns), BF16),
        in_specs=[vmem] * (2 + len(vectors)),
        out_specs=vmem,
        name="pack_near",
    )(qkv, out, *[vector.reshape(1, -1) for vector in vectors])


def unpack_small(weights, count, width, wider):
    rows = width // count
    share, long_share = rows, wider // count
    used = -(-(8 * share + long_share) // LANES)

    def body(block_ref, vectors_ref, long_ref):
        block = wide(block_ref[...]).reshape(count, rows, LANES)
        flat = [low(block[:, line, :]) for line in range(used)]

        def spread(shift, period, columns):
            total = jnp.zeros((count, columns), F32)
            for line in range(used):
                pick = same(LANES, columns, shift - line * LANES, period)
                total = total + dot(flat[line], low(pick.astype(F32)))
            mine = jnp.where(owned(count, columns, period), total, 0.0)
            return jnp.sum(mine, axis=0, keepdims=True)

        for v in range(8):
            vectors_ref[v : v + 1, :] = spread(v * share, share, width)
        long_ref[...] = spread(8 * share, long_share, wider)

    return pl.pallas_call(
        body,
        grid=(1,),
        out_shape=(jax.ShapeDtypeStruct((8, width), F32), jax.ShapeDtypeStruct((1, wider), F32)),
        in_specs=[pl.BlockSpec((width, LANES), lambda i: (0, weights.shape[1] // LANES - 1))],
        out_specs=(
            pl.BlockSpec((8, width), lambda i: (0, 0)),
            pl.BlockSpec((1, wider), lambda i: (0, 0)),
        ),
        name="unpack_small",
    )(weights)


def normalized(value):
    centred = value - jnp.mean(value, axis=-1, keepdims=True)
    scale = lax.rsqrt(jnp.mean(centred * centred, axis=-1, keepdims=True) + EPSILON)
    return centred * scale, scale


def norm_back(grad, unit, scale, gain):
    inner = grad * gain
    average = jnp.mean(inner, axis=-1, keepdims=True)
    along = jnp.mean(inner * unit, axis=-1, keepdims=True)
    return scale * (inner - average - unit * along)


def column_sums(value):
    return jnp.sum(value, axis=0, keepdims=True)


def halves():
    lane = lax.broadcasted_iota(jnp.int32, (1, PAIR), 1)
    first = low((lane < HEAD_DIM).astype(F32))
    return first, low((lane >= HEAD_DIM).astype(F32))


def mask_of(across, down):
    slots = across.shape[1]
    row = lax.broadcasted_iota(jnp.int32, (slots, slots), 0)
    column = lax.broadcasted_iota(jnp.int32, (slots, slots), 1)
    allowed = ((down == across) & (down > 0)) | (row == column)
    return jnp.where(allowed, 0.0, BLOCKED)


def spread(product, rows, count, me, keep, send):
    if rows % 8 == 0:

        def place(slot, carry):
            for c, out in enumerate((keep, send)):
                start = pl.multiple_of((me ^ (2 * slot + c)) * rows, 8)
                out[slot] = low(product[pl.ds(start, rows), :])
            return carry

        lax.fori_loop(0, count // 2, place, 0, unroll=min(4, count // 2))
        return
    for couple in range(count // 2):
        slot = couple ^ (me // 2)
        even = low(product[2 * couple * rows : (2 * couple + 1) * rows, :])
        odd = low(product[(2 * couple + 1) * rows : (2 * couple + 2) * rows, :])
        keep[slot] = jnp.where(me % 2 == 0, even, odd)
        send[slot] = jnp.where(me % 2 == 0, odd, even)


def attend(x, across, down, weights, vectors):
    tokens, width = x.shape
    slots = across.shape[2]
    rows = tokens // slots
    heads = width // HEAD_DIM

    def body(x_ref, across_ref, down_ref, w_ref, vec_ref, first_ref, qkv_ref, ctx_ref, lse_ref, mid_ref, second_ref):
        value = wide(x_ref[...])
        unit, _ = normalized(value)
        first = low(unit * vec_ref[0:1, :] + vec_ref[1:2, :])
        first_ref[...] = first
        for part in range(3):
            product = dot(first, w_ref[:, part * width : (part + 1) * width])
            if part != 1:
                product = product + vec_ref[2 + part // 2 : 3 + part // 2, :]
            qkv_ref[:, part * width : (part + 1) * width] = low(product)
        bias = mask_of(across_ref[0], down_ref[...])
        masks = halves()
        place = lax.broadcasted_iota(jnp.int32, (slots, heads), 1)

        def couple(pair, found):
            def lanes(part):
                return pl.ds(pl.multiple_of(part * width + pair * PAIR, PAIR), PAIR)

            q, k, v = (qkv_ref[:, lanes(part)] for part in range(3))
            context = jnp.zeros((slots, PAIR), F32)
            for side in range(2):
                scores = dot(q * masks[side], k, 1, 1) * HEAD_DIM**-0.5 + bias
                highest = jnp.max(scores, axis=-1, keepdims=True)
                powers = jnp.exp(scores - highest)
                total = jnp.sum(powers, axis=-1, keepdims=True)
                probs = low(powers * (1.0 / total))
                context = context + dot(probs, v * masks[side])
                found = jnp.where(place == 2 * pair + side, highest + jnp.log(total), found)
            ctx_ref[:, lanes(0)] = low(context)
            return found

        def several(step, found):
            for offset in range(GROUP):
                found = couple(step * GROUP + offset, found)
            return found

        lse_ref[...] = lax.fori_loop(
            0, heads // 2 // GROUP, several, jnp.zeros((slots, heads), F32)
        )
        attention = dot(ctx_ref[...], w_ref[:, 3 * width : 4 * width]) + vec_ref[4:5, :]
        middle = value + attention
        mid_ref[...] = middle
        unit, _ = normalized(middle)
        second_ref[...] = low(unit * vec_ref[5:6, :] + vec_ref[6:7, :])

    def row(columns):
        return pl.BlockSpec((slots, columns), lambda i: (i, 0))

    def whole(array):
        return pl.BlockSpec(array.shape, lambda i: (0, 0), pipeline_mode=pl.Buffered(1))

    shapes = [(width, BF16), (3 * width, BF16), (width, BF16), (heads, F32), (width, F32), (width, BF16)]
    return pl.pallas_call(
        body,
        grid=(rows,),
        out_shape=tuple(jax.ShapeDtypeStruct((tokens, c), t) for c, t in shapes),
        in_specs=[
            row(width),
            pl.BlockSpec((1, 1, slots), lambda i: (i, 0, 0)),
            row(1),
            whole(weights),
            whole(vectors),
        ],
        out_specs=tuple(row(c) for c, _ in shapes),
        compiler_params=pltpu.CompilerParams(vmem_limit_bytes=VMEM_LIMIT),
        cost_estimate=pl.CostEstimate(
            flops=2 * tokens * width * width * 4 + 4 * rows * heads * slots * slots * HEAD_DIM,
            transcendentals=rows * heads * slots * slots,
            bytes_accessed=30 << 20,
        ),
        name="attend",
    )(x, across, down, weights, vectors)


def feed_forward(second, upstream, middle, up, down, vectors, long_bias, count):
    tokens, width = second.shape
    wider = up.shape[1]
    tile = FF_TILE
    steps = wider // tile
    down_rows = wider // count
    group = tile // down_rows

    def body(
        id_ref, second_ref, grad_ref, mid_ref, up_ref, down_ref, vec_ref, bias_ref,
        out_ref, back_ref, down_keep, down_send, long_ref, rows_ref,
        out_sum, down_product,
    ):
        step = pl.program_id(0)
        me = id_ref[0]

        @pl.when(step == 0)
        def _():
            out_sum[...] = jnp.zeros_like(out_sum)

        grads = grad_ref[...]
        hidden = dot(second_ref[...], up_ref[...]) + bias_ref[...]
        below = 0.5 * (1.0 + lax.erf(hidden * 0.7071067811865476))
        active = low(hidden * below)
        slope = below + hidden * (jnp.exp(hidden * hidden * -0.5) * 0.3989422804014327)
        back = low(dot(grads, down_ref[...], 1, 1) * slope)
        back_ref[...] = back
        long_ref[...] = column_sums(wide(back))
        out_sum[...] += dot(active, down_ref[...])
        down_product[...] = dot(active, grads, 0, 0)
        spread(down_product, down_rows, group, me % group, down_keep, down_send)

        @pl.when(step == steps - 1)
        def _():
            out_ref[...] = low(mid_ref[...] + (out_sum[...] + vec_ref[7:8, :]))
            rows_ref[...] = jnp.broadcast_to(column_sums(wide(grads)), (8, width))

    def whole(array):
        return pl.BlockSpec(array.shape, lambda i, m: (0, 0), pipeline_mode=pl.Buffered(1))

    half = count // 2
    down_spec = pl.BlockSpec((group // 2, down_rows, width), lambda i, m: (i ^ (m[0] // group), 0, 0))
    return pl.pallas_call(
        body,
        grid_spec=pltpu.PrefetchScalarGridSpec(
            num_scalar_prefetch=1,
            grid=(steps,),
            in_specs=[
                whole(second), whole(upstream), whole(middle),
                pl.BlockSpec((width, tile), lambda i, m: (0, i)),
                pl.BlockSpec((tile, width), lambda i, m: (i, 0)),
                whole(vectors),
                pl.BlockSpec((1, tile), lambda i, m: (0, i)),
            ],
            out_specs=(
                pl.BlockSpec((tokens, width), lambda i, m: (0, 0)),
                pl.BlockSpec((tokens, tile), lambda i, m: (0, i)),
                down_spec, down_spec,
                pl.BlockSpec((1, tile), lambda i, m: (0, i)),
                pl.BlockSpec((8, width), lambda i, m: (0, 0)),
            ),
            scratch_shapes=[pltpu.VMEM((tokens, width), F32), pltpu.VMEM((tile, width), F32)],
        ),
        out_shape=(
            jax.ShapeDtypeStruct((tokens, width), BF16),
            jax.ShapeDtypeStruct((tokens, wider), BF16),
            jax.ShapeDtypeStruct((half, down_rows, width), BF16),
            jax.ShapeDtypeStruct((half, down_rows, width), BF16),
            jax.ShapeDtypeStruct((1, wider), F32),
            jax.ShapeDtypeStruct((8, width), F32),
        ),
        compiler_params=pltpu.CompilerParams(vmem_limit_bytes=VMEM_LIMIT),
        cost_estimate=pl.CostEstimate(
            flops=8 * tokens * width * wider, transcendentals=2 * tokens * wider,
            bytes_accessed=30 << 20,
        ),
        name="feed_forward",
    )(my_id(), second, upstream, middle, up, down, vectors, long_bias)


def feed_back(second, back, upstream, middle, up, vectors, count):
    tokens, width = second.shape
    wider = up.shape[1]
    tile = FF_TILE
    steps = wider // tile
    up_rows = width // count

    def body(
        id_ref, second_ref, back_ref, grad_ref, mid_ref, up_ref, vec_ref,
        dmid_ref, up_keep, up_send, rows_ref,
        back_sum, second_turned, up_product,
    ):
        step = pl.program_id(0)

        @pl.when(step == 0)
        def _():
            second_turned[...] = second_ref[...].T
            back_sum[...] = jnp.zeros_like(back_sum)

        back_sum[...] += dot(back_ref[...], up_ref[...], 1, 1)
        up_product[...] = dot(second_turned[...], back_ref[...])
        spread(up_product, up_rows, count, id_ref[0], up_keep, up_send)

        @pl.when(step == steps - 1)
        def _():
            unit, scale = normalized(mid_ref[...])
            da = back_sum[...]
            dmid_ref[...] = wide(grad_ref[...]) + norm_back(da, unit, scale, vec_ref[5:6, :])
            rows_ref[...] = jnp.zeros_like(rows_ref)
            rows_ref[0:1, :] = column_sums(da * unit)
            rows_ref[1:2, :] = column_sums(da)

    def whole(array):
        return pl.BlockSpec(array.shape, lambda i, m: (0, 0), pipeline_mode=pl.Buffered(1))

    half = count // 2
    up_spec = pl.BlockSpec((half, up_rows, tile), lambda i, m: (0, 0, i))
    return pl.pallas_call(
        body,
        grid_spec=pltpu.PrefetchScalarGridSpec(
            num_scalar_prefetch=1,
            grid=(steps,),
            in_specs=[
                whole(second),
                pl.BlockSpec((tokens, tile), lambda i, m: (0, i)),
                whole(upstream), whole(middle),
                pl.BlockSpec((width, tile), lambda i, m: (0, i)),
                whole(vectors),
            ],
            out_specs=(
                pl.BlockSpec((tokens, width), lambda i, m: (0, 0)),
                up_spec, up_spec,
                pl.BlockSpec((8, width), lambda i, m: (0, 0)),
            ),
            scratch_shapes=[
                pltpu.VMEM((tokens, width), F32), pltpu.VMEM((width, tokens), BF16),
                pltpu.VMEM((width, tile), F32),
            ],
        ),
        out_shape=(
            jax.ShapeDtypeStruct((tokens, width), F32),
            jax.ShapeDtypeStruct((half, up_rows, wider), BF16),
            jax.ShapeDtypeStruct((half, up_rows, wider), BF16),
            jax.ShapeDtypeStruct((8, width), F32),
        ),
        compiler_params=pltpu.CompilerParams(vmem_limit_bytes=VMEM_LIMIT),
        cost_estimate=pl.CostEstimate(
            flops=4 * tokens * width * wider, transcendentals=tokens, bytes_accessed=25 << 20
        ),
        name="feed_back",
    )(my_id(), second, back, upstream, middle, up, vectors)


def attend_back(x, across, down, weights, vectors, qkv, lse, dmid):
    tokens, width = x.shape
    slots = across.shape[2]
    rows = tokens // slots
    heads = width // HEAD_DIM

    def body(
        x_ref, across_ref, down_ref, w_ref, vec_ref, qkv_ref, lse_ref, dmid_ref,
        dx_ref, dqkv_ref, dattn_ref, sums,
        dctx,
    ):
        @pl.when(pl.program_id(0) == 0)
        def _():
            sums[...] = jnp.zeros_like(sums)

        middle_grad = dmid_ref[...]
        dattn = low(middle_grad)
        dattn_ref[...] = dattn
        dctx[...] = low(dot(dattn, w_ref[:, 3 * width : 4 * width], 1, 1))
        bias = mask_of(across_ref[0], down_ref[...])
        masks = halves()
        place = lax.broadcasted_iota(jnp.int32, (slots, heads), 1)

        def couple(pair):
            def lanes(part):
                return pl.ds(pl.multiple_of(part * width + pair * PAIR, PAIR), PAIR)

            mine = pl.ds(0, slots)
            q, k, v = (qkv_ref[mine, lanes(part)] for part in range(3))
            dout = dctx[:, lanes(0)]
            dq = jnp.zeros((slots, PAIR), F32)
            dk = jnp.zeros((slots, PAIR), F32)
            dv = jnp.zeros((slots, PAIR), F32)
            for side in range(2):
                kept = jnp.where(place == 2 * pair + side, lse_ref[...], 0.0)
                kept = jnp.sum(kept, axis=-1, keepdims=True)
                q_half, dout_half = q * masks[side], dout * masks[side]
                scores = dot(q_half, k, 1, 1) * HEAD_DIM**-0.5 + bias
                probs = jnp.exp(scores - kept)
                dprobs = dot(dout_half, v, 1, 1)
                weighted = probs * dprobs
                dscores = low(weighted - probs * jnp.sum(weighted, axis=-1, keepdims=True))
                dv = dv + dot(low(probs), dout_half, 0, 0)
                dq = dq + dot(dscores, k * masks[side])
                dk = dk + dot(dscores, q_half, 0, 0)
            dqkv_ref[:, lanes(0)] = low(dq * HEAD_DIM**-0.5)
            dqkv_ref[:, lanes(1)] = low(dk * HEAD_DIM**-0.5)
            dqkv_ref[:, lanes(2)] = low(dv)

        def several(step, carry):
            for offset in range(GROUP):
                couple(step * GROUP + offset)
            return carry

        lax.fori_loop(0, heads // 2 // GROUP, several, 0)
        dfirst = jnp.zeros((slots, width), F32)
        for p in range(3):
            part = slice(p * width, (p + 1) * width)
            dfirst = dfirst + dot(dqkv_ref[:, part], w_ref[:, part], 1, 1)
        unit, scale = normalized(wide(x_ref[...]))
        dx_ref[...] = low(middle_grad + norm_back(dfirst, unit, scale, vec_ref[0:1, :]))
        sums[0:1, :] += column_sums(dfirst * unit)
        sums[1:2, :] += column_sums(dfirst)
        sums[2:3, :] += column_sums(wide(dqkv_ref[:, :width]))
        sums[3:4, :] += column_sums(wide(dqkv_ref[:, 2 * width :]))
        sums[4:5, :] += column_sums(wide(dattn))

    def row(columns):
        return pl.BlockSpec((slots, columns), lambda i: (i, 0))

    def whole(array):
        return pl.BlockSpec(array.shape, lambda i: (0, 0), pipeline_mode=pl.Buffered(1))

    return pl.pallas_call(
        body,
        grid=(rows,),
        in_specs=[
            row(width),
            pl.BlockSpec((1, 1, slots), lambda i: (i, 0, 0)),
            row(1), whole(weights), whole(vectors), row(3 * width), row(heads), row(width),
        ],
        out_specs=(
            row(width), row(3 * width), row(width), pl.BlockSpec((8, width), lambda i: (0, 0))
        ),
        scratch_shapes=[pltpu.VMEM((slots, width), BF16)],
        out_shape=(
            jax.ShapeDtypeStruct((tokens, width), BF16),
            jax.ShapeDtypeStruct((tokens, 3 * width), BF16),
            jax.ShapeDtypeStruct((tokens, width), BF16),
            jax.ShapeDtypeStruct((8, width), F32),
        ),
        compiler_params=pltpu.CompilerParams(vmem_limit_bytes=VMEM_LIMIT),
        cost_estimate=pl.CostEstimate(
            flops=2 * tokens * width * width * 4 + 10 * rows * heads * slots * slots * HEAD_DIM,
            transcendentals=rows * heads * slots * slots,
            bytes_accessed=25 << 20,
        ),
        name="attend_back",
    )(x, across, down, weights, vectors, qkv, lse, dmid)


def attend_weights(first, dqkv, context, dattn, sums, mid_rows, down_rows, long_row, count):
    tokens, width = first.shape
    wider = long_row.shape[1]
    share, long_share = width // count, wider // count
    used = -(-(8 * share + long_share) // LANES)

    def body(
        id_ref, first_ref, dqkv_ref, ctx_ref, dattn_ref, sums_ref, mid_ref, last_ref, long_ref,
        keep_ref, send_ref, product,
    ):
        me = id_ref[0]
        turned = first_ref[...].T
        for p in range(4):
            part = slice(p * width, (p + 1) * width)
            if p < 3:
                product[...] = dot(turned, dqkv_ref[:, part])
            else:
                product[...] = dot(ctx_ref[...], dattn_ref[...], 0, 0)

            spread(
                product, share, count, me, keep_ref.at[:, :, part], send_ref.at[:, :, part]
            )

        def fold(row, shift, period):
            columns = row.shape[1]
            mine = low(jnp.where(owned(count, columns, period), row, 0.0))
            found = []
            for line in range(used):
                pick = same(LANES, columns, shift - line * LANES, period)
                found.append(dot(mine, low(pick.astype(F32)), 1, 1))
            return found

        lines = fold(long_ref[...], 8 * share, long_share)
        for v in range(8):
            source, line = ((sums_ref, v), (mid_ref, v - 5), (last_ref, 0))[(v > 4) + (v > 6)]
            row = source[line : line + 1, :]
            lines = [old + new for old, new in zip(lines, fold(row, v * share, share))]
        number = lax.broadcasted_iota(jnp.int32, (share, LANES), 0)

        def block_of(owner):
            block = jnp.zeros((share, LANES), F32)
            for line in range(used):
                block = jnp.where(number == line, lines[line][owner : owner + 1, :], block)
            return low(block)

        for couple in range(count // 2):
            slot = couple ^ (me // 2)
            even, odd = block_of(2 * couple), block_of(2 * couple + 1)
            keep_ref[slot, :, 4 * width :] = jnp.where(me % 2 == 0, even, odd)
            send_ref[slot, :, 4 * width :] = jnp.where(me % 2 == 0, odd, even)

    block = (count // 2, share, 4 * width + LANES)
    vmem = pl.BlockSpec(memory_space=pltpu.VMEM)
    return pl.pallas_call(
        body,
        in_specs=[pl.BlockSpec(memory_space=pltpu.SMEM)] + [vmem] * 8,
        out_specs=(vmem, vmem),
        out_shape=(jax.ShapeDtypeStruct(block, BF16), jax.ShapeDtypeStruct(block, BF16)),
        scratch_shapes=[pltpu.VMEM((width, width), F32)],
        compiler_params=pltpu.CompilerParams(vmem_limit_bytes=VMEM_LIMIT),
        cost_estimate=pl.CostEstimate(
            flops=2 * tokens * width * width * 4, transcendentals=0, bytes_accessed=15 << 20
        ),
        name="attend_weights",
    )(my_id(), first, dqkv, context, dattn, sums, mid_rows, down_rows, long_row)


def shards(
    layer_input, segments, cotangent, pre_gain, pre_shift, w_qkv, b_query, b_value, w_out, b_out,
    mid_gain, mid_shift, w_up, b_up, w_down, b_down,
):
    row_count, slot_count, width = layer_input.shape
    tokens = row_count * slot_count
    share, long_share = pre_gain.shape[0], b_up.shape[0]
    count = width // share
    small = [pre_gain, pre_shift, b_query, b_value, b_out, mid_gain, mid_shift, b_down, b_up]
    near = pack_near(w_qkv, w_out, small)

    near_pieces = gather_chips(near, count)
    up_pieces = gather_chips(low(w_up), count)
    down_pieces = gather_chips(low(w_down), count)
    near_all = gather_core(near_pieces, count)
    near_full = lay_out(near_all, count)

    x = layer_input.reshape(tokens, width)
    grads = cotangent.reshape(tokens, width)
    across = segments.reshape(row_count, 1, slot_count)
    down = segments.reshape(tokens, 1)
    vectors, long_bias = unpack_small(near_full, count, width, count * long_share)
    first, qkv, context, lse, middle, second = attend(x, across, down, near_full, vectors)
    up_full = lay_out(gather_core(up_pieces, count), count)
    down_full = lay_out(gather_core(down_pieces, count), count)
    result, back, down_keep, down_send, long_row, down_row = feed_forward(
        second, grads, middle, up_full, down_full, vectors, long_bias, count
    )
    dmid, up_keep, up_send, mid_rows = feed_back(
        second, back, grads, middle, up_full, vectors, count
    )
    down_total = reduce_blocks(down_keep, down_send, count)
    up_total = reduce_blocks(up_keep, up_send, count)
    dx, dqkv, dattn, sums = attend_back(x, across, down, near_full, vectors, qkv, lse, dmid)
    keep, send = attend_weights(
        first, dqkv, context, dattn, sums, mid_rows, down_row, long_row, count
    )
    total = reduce_blocks(keep, send, count)
    used = -(-(8 * share + long_share) // LANES)
    flat = total[:used, 4 * width :].reshape(-1)
    vector_grads = [flat[v * share : (v + 1) * share] for v in range(8)]
    return (
        result.reshape(layer_input.shape),
        dx.reshape(layer_input.shape),
        vector_grads[0],
        vector_grads[1],
        total[:, : 3 * width],
        vector_grads[2],
        vector_grads[3],
        total[:, 3 * width : 4 * width],
        vector_grads[4],
        vector_grads[5],
        vector_grads[6],
        up_total,
        flat[8 * share : 8 * share + long_share],
        down_total,
        vector_grads[7],
    )


def solution(mesh):
    line, table = P(AXIS), P(AXIS, None)
    cube = P(AXIS, None, None)
    return jax.shard_map(
        shards,
        mesh=mesh,
        in_specs=(
            cube, table, cube, line, line, table, line, line, table, line, line, line, table, line,
            table, line,
        ),
        out_specs=(
            cube, cube, line, line, table, line, line, table, line, line, line, table, line, table,
            line,
        ),
        check_vma=False,
    )
```
